32 devices in a mesh: ctx: 8 (over z, x), dp: 4 (over y, core).
Axes of the slice: x: 2, y: 2, z: 4, core: 2. Of those that a mesh axis runs over, the one named last changes fastest.
Arguments:
- query_in: bfloat16 [4, 2048, 4096], P('dp', 'ctx'), may hold values from -6 to 6
- key_in: bfloat16 [4, 2048, 512], P('dp', 'ctx'), may hold values from -6 to 6
- value_rows_input: bfloat16 [4, 2048, 512], P('dp', 'ctx'), may hold values from -6 to 6
- grad_out: bfloat16 [4, 2048, 4096], P('dp', 'ctx'), may hold values from -12 to 12
- query_bias: float32 [4096], replicated, may hold values from -1.5 to 1.5
- key_blocks: int32 [4, 16, 6], P('dp'), may hold values from -1 to 15, as said below
- trace_len: int32 [4], P('dp'), may hold values from 1024 to 2048, as said below
Outputs:
- grad_query: bfloat16 [4, 2048, 4096], P('dp', 'ctx')
- grad_key: bfloat16 [4, 2048, 512], P('dp', 'ctx')
- grad_value: bfloat16 [4, 2048, 512], P('dp', 'ctx')
- bias_grad: float32 [4096], replicated
The draws below stay inside these ranges and needn't reach their ends.
Inputs may be any that keep to these rules, and one draw needn't show every extreme that they name: `key_blocks`: blocks are numbered by position. Entry 2 + d of query block q's list is q - d or -1, and entry 2 is always q; entry r < 2 is r or -1, and -1 whenever r >= q - 3. `trace_len`: some trace has 2048 tokens and some 2048 // 2.
All inputs are finite; a program needn't handle non-finite values.
Results may differ from the reference program's by a relative error of at most 0.011.
The reference program's roundings to bfloat16 on the way (of `queries`, `probs_low` and `grad_scores`) count: a program that leaves them out, or rounds other values in their place, can miss the bound.
Values may be sent and summed in bfloat16 or wider, within the bound.
No kernel may reach another device: no remote copies, remote signals or barrier semaphores. Data moves between devices by JAX's collectives and lax.ppermute only.
A program may use at most 128 MiB of HBM per device.

```python
import math
import jax
import jax.numpy as jnp
from jax import lax

QUERY_HEADS = 32
KEY_VALUE_HEADS = 4
HEAD_SIZE = 128
BLOCK = 128
PROMPT = 2
WINDOW = 3
TRACE_COUNT = 4
NBLK = 16
TRACE_LENGTH = 2048
N_CTX = 8


def draw_query_in(key, part):
    base_value = jnp.clip(jax.random.normal(jax.random.fold_in(key, 1), (TRACE_COUNT, TRACE_LENGTH, QUERY_HEADS * HEAD_SIZE), jnp.float32), -6.0, 6.0)
    return base_value.astype(jnp.bfloat16)


def draw_key_in(key, part):
    base_value = jnp.clip(jax.random.normal(jax.random.fold_in(key, 2), (TRACE_COUNT, TRACE_LENGTH, KEY_VALUE_HEADS * HEAD_SIZE), jnp.float32), -6.0, 6.0)
    return base_value.astype(jnp.bfloat16)


def draw_grad_out(key, part):
    ramp = 1.0 + 2.0 * jnp.arange(TRACE_LENGTH, dtype=jnp.float32) / (TRACE_LENGTH - 1)
    base_value = jnp.clip(jax.random.normal(jax.random.fold_in(key, 3), (TRACE_COUNT, TRACE_LENGTH, QUERY_HEADS * HEAD_SIZE), jnp.float32), -4.0, 4.0)
    return (base_value * ramp[None, :, None]).astype(jnp.bfloat16)


def block_plan(key):
    block_idx = jnp.arange(NBLK, dtype=jnp.int32)
    starts = (jax.random.randint(jax.random.fold_in(key, 202), (TRACE_COUNT, NBLK), 0, 3, jnp.int32) == 0) & (block_idx >= PROMPT)[None]
    starts = starts | (block_idx == PROMPT)[None]
    step_id = jnp.cumsum(starts.astype(jnp.int32), axis=1)
    query_blk = block_idx[None, :, None]

    def permitted(key_blk):
        safe = jnp.clip(key_blk, 0, NBLK - 1)[0]
        key_step = jax.vmap(lambda row: row[safe])(step_id)
        query_step = step_id[:, :, None]
        nearby = (key_blk >= query_blk - WINDOW) & (key_step >= query_step - 1)
        return (key_blk >= 0) & (key_blk <= query_blk) & ((key_blk < PROMPT) | nearby)
    prompt_blk = jnp.broadcast_to(jnp.arange(PROMPT, dtype=jnp.int32)[None, None, :], (1, NBLK, PROMPT))
    window_blk = query_blk - jnp.arange(WINDOW + 1, dtype=jnp.int32)[None, None, :]
    prompt_slots = jnp.where(permitted(prompt_blk) & (prompt_blk < query_blk - WINDOW), prompt_blk, -1)
    window_slots = jnp.where(permitted(window_blk), window_blk, -1)
    return jnp.concatenate([prompt_slots, window_slots], axis=-1).astype(jnp.int32)


def draw_key_blocks(key, part):
    return block_plan(key)


def draw_trace_len(key, part):
    own_key = jax.random.fold_in(jax.random.fold_in(key, 201), part)
    lengths = jax.random.randint(jax.random.fold_in(own_key, 1), (TRACE_COUNT,), TRACE_LENGTH // 2, TRACE_LENGTH + 1, jnp.int32)
    order = jax.random.permutation(jax.random.fold_in(own_key, 2), TRACE_COUNT)
    lengths = lengths.at[order[0]].set(TRACE_LENGTH).at[order[1]].set(TRACE_LENGTH // 2)
    return lengths.astype(jnp.int32)


def shard_levels(stream_key, extent, pieces, least, high):
    factor_of, own = 1.0, jax.random.fold_in(stream_key, 6)
    for position, blocks in pieces:
        heights = jnp.exp(jax.random.uniform(jax.random.fold_in(own, position), (blocks,), jnp.float32, least / len(pieces), high / len(pieces)))
        factor_of = factor_of * jnp.repeat(heights, extent[position] // blocks).reshape([-1 if axis == position else 1 for axis in range(len(extent))])
    return factor_of


def normal_values(key, extent, deviation, limit, pieces=(), kind=jnp.bfloat16):
    entries = jax.random.normal(key, extent, jnp.float32) * deviation
    if len(pieces) > 0:
        entries = shard_levels(key, extent, pieces, -0.22, 0.18) * entries
    return jnp.clip(entries, min=-limit, max=limit).astype(kind)


def setup_inputs(seed: int = 0) -> dict:
    keys = jax.random.split(jax.random.key(seed), 8)
    query_in = draw_query_in(jax.random.fold_in(keys[7], 71), 0)
    key_in = draw_key_in(jax.random.fold_in(keys[7], 71), 0)
    value_rows_input = normal_values(keys[2], (TRACE_COUNT, TRACE_LENGTH, KEY_VALUE_HEADS * HEAD_SIZE), 1.0, 6.0, ((0, 4), (1, 8)))
    grad_out = draw_grad_out(jax.random.fold_in(keys[7], 71), 0)
    query_bias = normal_values(keys[4], (QUERY_HEADS * HEAD_SIZE,), 0.3, 1.5, (), jnp.float32)
    key_blocks = draw_key_blocks(jax.random.fold_in(keys[7], 71), 0)
    trace_len = draw_trace_len(jax.random.fold_in(keys[7], 71), 0)
    return {"query_in": query_in, "key_in": key_in, "value_rows_input": value_rows_input, "grad_out": grad_out, "query_bias": query_bias, "key_blocks": key_blocks, "trace_len": trace_len}


def unfold(stored):
    traces = stored.shape[0]
    split = stored.reshape(traces, N_CTX, 2, BLOCK, stored.shape[-1])
    return jnp.concatenate([split[:, :, 0], split[:, ::-1, 1]], axis=1)

def refold(blocks):
    traces = blocks.shape[0]
    first_half = blocks[:, :N_CTX]
    second_half = blocks[:, N_CTX:][:, ::-1]
    return jnp.stack([first_half, second_half], axis=2).reshape(traces, 2 * N_CTX * BLOCK, blocks.shape[-1])

def block_grads(queries, cand_keys, cand_vals, grad_rows, allowed):
    score_scale = HEAD_SIZE ** (-0.5)
    query_wide = queries.astype(jnp.float32)
    keys_wide = cand_keys.astype(jnp.float32)
    vals_wide = cand_vals.astype(jnp.float32)
    grad_wide = grad_rows.astype(jnp.float32)
    scores = score_scale * jnp.einsum('qkgd,skd->kgqs', query_wide, keys_wide)
    scores = jnp.where(allowed[None, None], scores, -1e+30)
    row_max = lax.optimization_barrier(jnp.max(scores, axis=-1, keepdims=True))
    probs = jnp.where(allowed[None, None], jnp.exp(scores - row_max), 0.0)
    totals = lax.optimization_barrier(jnp.sum(probs, axis=-1, keepdims=True))
    row_live = jnp.any(allowed, axis=-1)[None, None, :, None]
    probs = probs / jnp.where(row_live, totals, 1.0)
    probs_low = lax.optimization_barrier(probs.astype(jnp.bfloat16))
    probs_wide = probs_low.astype(jnp.float32)
    attended = jnp.einsum('kgqs,skd->qkgd', probs_wide, vals_wide)
    row_dot = lax.optimization_barrier(jnp.sum(grad_wide * attended, axis=-1)).transpose(1, 2, 0)[..., None]
    grad_probs = jnp.einsum('qkgd,skd->kgqs', grad_wide, vals_wide)
    grad_low = lax.optimization_barrier((probs * (grad_probs - row_dot)).astype(jnp.bfloat16))
    grad_scores = grad_low.astype(jnp.float32)
    grad_query = score_scale * jnp.einsum('kgqs,skd->qkgd', grad_scores, keys_wide)
    grad_key = score_scale * jnp.einsum('kgqs,qkgd->skd', grad_scores, query_wide)
    grad_value = jnp.einsum('kgqs,qkgd->skd', probs_wide, grad_wide)
    return (grad_query, grad_key, grad_value)

def reference(query_in, key_in, value_rows_input, grad_out, query_bias, key_blocks, trace_len):
    width_kv = key_in.shape[-1]
    width_q = query_in.shape[-1]
    heads_kv = width_kv // HEAD_SIZE
    group_size = width_q // width_kv
    cand_count = PROMPT + WINDOW + 1
    nblocks = 2 * N_CTX

    def one_trace(packed):
        query_t, key_t, value_t, grad_t, block_rows, length = packed
        queries = (query_t.astype(jnp.float32) + query_bias).astype(jnp.bfloat16)

        def visit(carry, block_idx):
            key_sum, value_sum, bias_sum = carry
            key_ids = jnp.concatenate([jnp.arange(PROMPT, dtype=jnp.int32), block_idx - jnp.arange(WINDOW + 1, dtype=jnp.int32)])
            safe_ids = jnp.clip(key_ids, 0, nblocks - 1)
            cand_keys = key_t[safe_ids].reshape(cand_count * BLOCK, heads_kv, HEAD_SIZE)
            cand_vals = value_t[safe_ids].reshape(cand_count * BLOCK, heads_kv, HEAD_SIZE)
            listed = block_rows[block_idx] >= 0
            prompt_ok = jnp.concatenate([jnp.arange(PROMPT, dtype=jnp.int32) < block_idx - WINDOW, jnp.ones((WINDOW + 1,), jnp.bool_)])
            block_ok = jnp.repeat(listed & prompt_ok, BLOCK)
            key_pos = (key_ids[:, None] * BLOCK + jnp.arange(BLOCK, dtype=jnp.int32)[None]).reshape(-1)
            query_pos = block_idx * BLOCK + jnp.arange(BLOCK, dtype=jnp.int32)
            allowed = block_ok[None] & (key_pos[None] <= query_pos[:, None]) & (key_pos[None] < length) & (query_pos[:, None] < length)
            grad_query, grad_key, grad_value = block_grads(queries[block_idx].reshape(BLOCK, heads_kv, group_size, HEAD_SIZE), cand_keys, cand_vals, grad_t[block_idx].reshape(BLOCK, heads_kv, group_size, HEAD_SIZE), allowed)
            key_sum = key_sum.at[safe_ids].add(grad_key.reshape(cand_count, BLOCK, width_kv))
            value_sum = value_sum.at[safe_ids].add(grad_value.reshape(cand_count, BLOCK, width_kv))
            flat_query = grad_query.reshape(BLOCK, width_q)
            bias_sum = bias_sum + lax.optimization_barrier(jnp.sum(flat_query, axis=0))
            return ((key_sum, value_sum, bias_sum), flat_query.astype(jnp.bfloat16))
        start = (jnp.zeros((nblocks, BLOCK, width_kv), jnp.float32), jnp.zeros((nblocks, BLOCK, width_kv), jnp.float32), jnp.zeros((width_q,), jnp.float32))
        (key_sum, value_sum, bias_sum), grad_blocks = lax.scan(visit, start, jnp.arange(nblocks, dtype=jnp.int32))
        return (grad_blocks, key_sum.astype(jnp.bfloat16), value_sum.astype(jnp.bfloat16), bias_sum)
    grad_q, grad_k, grad_v, bias_parts = lax.map(one_trace, (unfold(query_in), unfold(key_in), unfold(value_rows_input), unfold(grad_out), key_blocks, trace_len))
    bias_grad = lax.optimization_barrier(jnp.sum(bias_parts, axis=0)) / math.sqrt(TRACE_COUNT * TRACE_LENGTH)
    return (refold(grad_q), refold(grad_k), refold(grad_v), bias_grad)
```

```python
import functools
import math

import jax
import jax.numpy as jnp
from jax import lax
from jax.experimental import pallas as pl
from jax.experimental.pallas import tpu as pltpu
from jax.sharding import PartitionSpec as P

HEAD = 128
BLOCK = 128
PROMPT = 2
WINDOW = 3
CAND = PROMPT + WINDOW + 1

LOW, HIGH, L1, U1, L2, U2, EXTRA, L3, U3, SWAP, RELAY = range(11)


def relay_rounds(n):
    known = [0, 2, n // 2 - 1]
    missing = list(range(3, n // 2 - 1))
    rounds = []
    while missing:
        pairs = list(zip(known, missing))
        rounds.append(pairs)
        known = known + [b for _, b in pairs]
        missing = missing[len(pairs) :]
    return rounds


def plan(n):
    up1 = [(s, s + 1) for s in range(n - 1)]
    down1 = [(s, s - 1) for s in range(1, n)]
    up2 = [(s, s + 2) for s in range(n - 2)]
    ring2 = [(s, (s - 2) % n) for s in range(n)]
    down2 = [(s, s - 2) for s in range(2, n)]
    extra = [(0, 4), (1, 5), (n - 1, n - 2)]
    swap = [(1, 0)] + [(s, s ^ 1) for s in range(4, n)]
    relay = [
        [(2 * a + x, 2 * b + x) for a, b in pairs for x in range(2)] for pairs in relay_rounds(n)
    ]
    return up1, down1, up2, ring2, down2, extra, swap, relay


def send(value, pairs):
    return lax.ppermute(value, "ctx", pairs)


def send_back(value, pairs):
    return lax.ppermute(value, "ctx", [(b, a) for a, b in pairs])


def slots(r, n, half):
    def pick(default, *cases):
        out = default
        for cond, value in reversed(cases):
            out = jnp.where(cond, value, out)
        return out

    even = r % 2 == 0
    column = pick(RELAY, (r < 6, EXTRA), (r >= n - 2, U2))
    p0 = pick(
        jnp.where(even, column, SWAP), (r == 0, LOW), (r == 1, L1), (r == 2, L2), (r == 3, L3)
    )
    p1 = pick(
        jnp.where(even, SWAP, column), (r == 0, SWAP), (r == 1, LOW), (r == 2, L1), (r == 3, L2)
    )
    low = [LOW, L1, L2, L3]
    high = [
        HIGH,
        pick(U1, (r == n - 1, LOW)),
        pick(U2, (r == n - 2, EXTRA), (r == n - 1, L1)),
        pick(U3, (r == n - 2, LOW), (r == n - 1, L2)),
    ]
    return [p0, p1] + [jnp.where(half == 0, a, b) for a, b in zip(low, high)]


def attend_kernel(
    n, nbuf, heads, group, rank_ref, blocks_ref, len_ref, q_ref, g_ref, bias_ref, *refs
):
    bufs = refs[:nbuf]
    dq_ref, dbias_ref, own_ref = refs[nbuf : nbuf + 3]
    outs = refs[nbuf + 3 : nbuf + 3 + nbuf - 2]
    kv, acc, probs_buf, ds_buf = refs[nbuf + 3 + nbuf - 2 :]
    t, k, half = pl.program_id(0), pl.program_id(1), pl.program_id(2)
    r = rank_ref[0]
    scale = HEAD ** (-0.5)
    factor = scale * math.log2(math.e)
    block = jnp.where(half == 0, r, 2 * n - 1 - r)
    where_from = slots(r, n, half)
    base = (t * 2 * n + block) * CAND
    ok = []
    for c in range(CAND):
        listed = blocks_ref[base + c] >= 0
        if c < PROMPT:
            listed = listed & (c < block - WINDOW)
        ok.append(listed)

    @pl.when((k == 0) & (half == 0))
    def _():
        for i in range(nbuf):
            kv[i] = bufs[i][0]

    @pl.when(half == 0)
    def _():
        acc[...] = jnp.zeros_like(acc)

    keys = jnp.concatenate([kv[s, k] for s in where_from], axis=0)
    vals = jnp.concatenate([kv[s, heads + k] for s in where_from], axis=0)
    keys_t = keys.T
    queries, grads = [], []
    for g in range(group):
        cols = slice(g * HEAD, (g + 1) * HEAD)
        queries.append((q_ref[0, :, cols].astype(jnp.float32) + bias_ref[:, cols]).astype(jnp.bfloat16))
        grads.append(g_ref[0, :, cols])
    nt = (((1,), (1,)), ((), ()))
    width = 2 * BLOCK
    key_pos = lax.broadcasted_iota(jnp.int32, (BLOCK, width), 0)
    query_pos = lax.broadcasted_iota(jnp.int32, (BLOCK, width), 1) % BLOCK
    causal = key_pos <= query_pos
    live = block * BLOCK + query_pos[:1] < len_ref[t]
    for pair in range(group // 2):
        q_two = jnp.concatenate(queries[2 * pair : 2 * pair + 2], axis=0)
        g_two = jnp.concatenate(grads[2 * pair : 2 * pair + 2], axis=0)
        scores = lax.dot_general(keys, q_two, nt, preferred_element_type=jnp.float32)
        parts = []
        for c in range(CAND):
            part = scores[c * BLOCK : (c + 1) * BLOCK]
            if c == PROMPT:
                parts.append(jnp.where(causal, part, -1e30))
            else:
                parts.append(jnp.where(ok[c], part, -1e30))
        scores = jnp.concatenate(parts, axis=0)
        top = jnp.max(scores, axis=0, keepdims=True)
        probs = jnp.exp2((scores - top) * factor)
        total = jnp.sum(probs, axis=0, keepdims=True)
        probs = probs * jnp.where(live, 1.0 / total, 0.0)
        probs_low = probs.astype(jnp.bfloat16)
        grad_probs = lax.dot_general(vals, g_two, nt, preferred_element_type=jnp.float32)
        row_dot = jnp.sum(probs_low.astype(jnp.float32) * grad_probs, axis=0, keepdims=True)
        grad_scores = (probs * (grad_probs - row_dot)).astype(jnp.bfloat16)
        span = slice(pair * width, (pair + 1) * width)
        probs_buf[:, span] = probs_low
        ds_buf[:, span] = grad_scores
        dq = scale * jnp.dot(keys_t, grad_scores, preferred_element_type=jnp.float32)
        for i in range(2):
            cols = slice((2 * pair + i) * HEAD, (2 * pair + i + 1) * HEAD)
            dq_head = dq[:, i * BLOCK : (i + 1) * BLOCK].T
            dq_ref[0, :, cols] = dq_head.astype(jnp.bfloat16)
            row = jnp.sum(dq_head, axis=0, keepdims=True)

            @pl.when((half == 0) & (t == 0))
            def _():
                dbias_ref[:, cols] = row

            @pl.when((half != 0) | (t != 0))
            def _():
                dbias_ref[:, cols] += row

    q_all = jnp.concatenate(queries, axis=0)
    g_all = jnp.concatenate(grads, axis=0)
    dk = scale * jnp.dot(ds_buf[...], q_all, preferred_element_type=jnp.float32)
    dv = jnp.dot(probs_buf[...], g_all, preferred_element_type=jnp.float32)
    for c in range(CAND):
        rows = slice(c * BLOCK, (c + 1) * BLOCK)
        acc[where_from[c], 0] += dk[rows]
        acc[where_from[c], 1] += dv[rows]

    @pl.when(half == 1)
    def _():
        for i in range(2):
            own_ref[0, i, :, 0] = acc[i]
        for i, out in enumerate(outs):
            out[0, :, 0] = acc[i + 2].astype(out.dtype)


def attend(n, heads, group, rank, blocks, lens, query_in, grad_out, bias, bufs):
    traces = query_in.shape[0]
    nbuf = len(bufs)
    width = group * HEAD
    row_spec = pl.BlockSpec((1, BLOCK, width), lambda t, k, j, *_: (t, j, k))
    bias_spec = pl.BlockSpec((1, width), lambda t, k, j, *_: (0, k))
    buf_spec = pl.BlockSpec((1, 2 * heads, BLOCK, HEAD), lambda t, k, j, *_: (t, 0, 0, 0))
    own_spec = pl.BlockSpec(
        (1, 2, 2, 1, BLOCK, HEAD), lambda t, k, j, *_: (t, 0, 0, k, 0, 0)
    )
    out_spec = pl.BlockSpec((1, 2, 1, BLOCK, HEAD), lambda t, k, j, *_: (t, 0, k, 0, 0))
    out_shape = [
        jax.ShapeDtypeStruct(query_in.shape, jnp.bfloat16),
        jax.ShapeDtypeStruct((1, heads * width), jnp.float32),
        jax.ShapeDtypeStruct((traces, 2, 2, heads, BLOCK, HEAD), jnp.float32),
    ] + [jax.ShapeDtypeStruct((traces, 2, heads, BLOCK, HEAD), jnp.bfloat16)] * (nbuf - 2)
    return pl.pallas_call(
        functools.partial(attend_kernel, n, nbuf, heads, group),
        out_shape=out_shape,
        grid_spec=pltpu.PrefetchScalarGridSpec(
            num_scalar_prefetch=3,
            grid=(traces, heads, 2),
            in_specs=[row_spec, row_spec, bias_spec] + [buf_spec] * nbuf,
            out_specs=[row_spec, bias_spec, own_spec] + [out_spec] * (nbuf - 2),
            scratch_shapes=[
                pltpu.VMEM((nbuf, 2 * heads, BLOCK, HEAD), jnp.bfloat16),
                pltpu.VMEM((nbuf, 2, BLOCK, HEAD), jnp.float32),
                pltpu.VMEM((CAND * BLOCK, width), jnp.bfloat16),
                pltpu.VMEM((CAND * BLOCK, width), jnp.bfloat16),
            ],
        ),
        compiler_params=pltpu.CompilerParams(
            dimension_semantics=("arbitrary", "arbitrary", "arbitrary"),
            vmem_limit_bytes=56 * 1024 * 1024,
        ),
        name="attend",
    )(rank, blocks, lens, query_in, grad_out, bias, *bufs)


def butterfly(value, axis):
    count = lax.axis_size(axis)
    stride = 1
    while stride < count:
        value = value + lax.ppermute(value, axis, [(s, s ^ stride) for s in range(count)])
        stride *= 2
    return value


def body(query_in, key_in, value_rows_input, grad_out, query_bias, key_blocks, trace_len):
    n = lax.axis_size("ctx")
    assert n >= 8 and n & (n - 1) == 0
    r = lax.axis_index("ctx")
    traces, _, width_q = query_in.shape
    width_kv = key_in.shape[-1]
    heads = width_kv // HEAD
    group = width_q // width_kv
    up1, down1, up2, ring2, down2, extra, swap, relay = plan(n)

    halves = jnp.concatenate([key_in, value_rows_input], axis=-1).reshape(
        traces, 2, BLOCK, 2 * heads, HEAD
    )
    low = halves[:, 0].transpose(0, 2, 1, 3)
    high = halves[:, 1].transpose(0, 2, 1, 3)
    in_l1 = send(low, up1)
    in_u1 = send(high, down1)
    in_l2 = send(low, up2)
    in_u2 = send(jnp.where(r < 2, low, high), ring2)
    in_ex = send(low, extra)
    column = jnp.where(r < 2, low, jnp.where(r < 6, in_ex, in_u2))
    bufs_relay = []
    for pairs in relay:
        got = send(column, pairs)
        targets = functools.reduce(jnp.logical_or, [r == b for _, b in pairs])
        column = jnp.where(targets, got, column)
    if relay:
        bufs_relay = [column]
    in_l3 = send(in_l1, up2)
    in_u3 = send(jnp.where(r == n - 1, low, in_u1), down2)
    in_sw = send(column, swap)
    bufs = [low, high, in_l1, in_u1, in_l2, in_u2, in_ex, in_l3, in_u3, in_sw] + bufs_relay

    dq, dbias, own, *outs = attend(
        n,
        heads,
        group,
        r.reshape(1).astype(jnp.int32),
        key_blocks.reshape(-1),
        trace_len,
        query_in,
        grad_out,
        query_bias.reshape(1, -1),
        bufs,
    )
    d_l1, d_u1, d_l2, d_u2, d_ex, d_l3, d_u3, d_sw = outs[:8]
    f32 = jnp.float32
    bf16 = jnp.bfloat16

    def gate(cond, value):
        return jnp.where(cond, value.astype(f32), 0.0)

    back_l3 = send_back(d_l3, up2)
    back_u3 = send_back(d_u3, down2)
    back_sw = send_back(d_sw, swap)
    back_l2 = send_back(d_l2, up2)
    d_l1 = (d_l1.astype(f32) + back_l3.astype(f32)).astype(bf16)
    d_u1 = (d_u1.astype(f32) + gate(r != n - 1, back_u3)).astype(bf16)
    back_l1 = send_back(d_l1, up1)
    back_u1 = send_back(d_u1, down1)
    if relay:
        d_rl = outs[8].astype(f32) + gate((r >= 6) & (r < n - 2), back_sw)
        d_ex = d_ex.astype(f32) + gate((r >= 4) & (r < 6), back_sw)
        d_u2 = d_u2.astype(f32) + gate(r >= n - 2, back_sw)
        low_extra = jnp.zeros_like(d_rl)
        for pairs in reversed(relay):
            is_from = functools.reduce(jnp.logical_or, [r == b for _, b in pairs])
            got = send_back(jnp.where(is_from, d_rl, 0.0).astype(bf16), pairs).astype(f32)
            low_extra = low_extra + gate(r < 2, got)
            d_ex = d_ex + gate((r >= 4) & (r < 6), got)
            d_u2 = d_u2 + gate(r >= n - 2, got)
            d_rl = d_rl + gate((r >= 6) & (r < n - 2), got)
        d_ex = d_ex.astype(bf16)
        d_u2 = d_u2.astype(bf16)
    else:
        d_ex = (d_ex.astype(f32) + gate((r >= 4) & (r < 6), back_sw)).astype(bf16)
        d_u2 = (d_u2.astype(f32) + gate(r >= n - 2, back_sw)).astype(bf16)
    back_ex = send_back(d_ex, extra)
    back_u2 = send_back(d_u2, ring2)

    low_grad = own[:, 0] + back_l1.astype(f32) + back_l2.astype(f32) + back_ex.astype(f32)
    low_grad = low_grad + gate(r < 2, back_u2) + gate(r == n - 1, back_u3) + gate(r == 1, back_sw)
    if relay:
        low_grad = low_grad + low_extra
    high_grad = own[:, 1] + back_u1.astype(f32) + gate(r >= 2, back_u2)
    both = jnp.stack([low_grad, high_grad], axis=1).astype(bf16)
    both = both.transpose(2, 0, 1, 4, 3, 5).reshape(2, traces, 2 * BLOCK, width_kv)
    bias_total = butterfly(butterfly(dbias.reshape(-1), "dp"), "ctx")
    rows = traces * lax.axis_size("dp") * 2 * BLOCK * n
    return dq, both[0], both[1], bias_total / math.sqrt(rows)


def solution(mesh):
    return jax.shard_map(
        body,
        mesh=mesh,
        in_specs=(
            P("dp", "ctx", None),
            P("dp", "ctx", None),
            P("dp", "ctx", None),
            P("dp", "ctx", None),
            P(),
            P("dp", None, None),
            P("dp"),
        ),
        out_specs=(P("dp", "ctx", None), P("dp", "ctx", None), P("dp", "ctx", None), P()),
        check_vma=False,
    )
```

```python
import functools
import math

import jax
import jax.numpy as jnp
from jax import lax
from jax.experimental import pallas as pl
from jax.experimental.pallas import tpu as pltpu

from jax.sharding import PartitionSpec as P


HEAD = 128
BLOCK = 128
PROMPT = 2
WINDOW = 3
CAND = PROMPT + WINDOW + 1

LOW, HIGH, L1, U1, L2, U2, EXTRA, L3, U3, SWAP, RELAY = range(11)


def relay_rounds(n):
    known = [0, 2, n // 2 - 1]
    missing = list(range(3, n // 2 - 1))
    rounds = []
    while missing:
        pairs = list(zip(known, missing))
        rounds.append(pairs)
        known = known + [b for _, b in pairs]
        missing = missing[len(pairs) :]
    return rounds


def plan(n):
    up1 = [(s, s + 1) for s in range(n - 1)]
    down1 = [(s, s - 1) for s in range(1, n)]
    up2 = [(s, s + 2) for s in range(n - 2)]
    ring2 = [(s, (s - 2) % n) for s in range(n)]
    down2 = [(s, s - 2) for s in range(2, n)]
    extra = [(0, 4), (1, 5), (n - 1, n - 2)]
    swap = [(1, 0)] + [(s, s ^ 1) for s in range(4, n)]
    relay = [
        [(2 * a + x, 2 * b + x) for a, b in pairs for x in range(2)] for pairs in relay_rounds(n)
    ]
    return up1, down1, up2, ring2, down2, extra, swap, relay


def send(value, pairs):
    return lax.ppermute(value, "ctx", pairs)


def send_back(value, pairs):
    return lax.ppermute(value, "ctx", [(b, a) for a, b in pairs])


def slots(r, n):
    def pick(default, *cases):
        out = default
        for cond, value in reversed(cases):
            out = jnp.where(cond, value, out)
        return out

    even = r % 2 == 0
    column = pick(RELAY, (r < 6, EXTRA), (r >= n - 2, U2))
    p0 = pick(
        jnp.where(even, column, SWAP), (r == 0, LOW), (r == 1, L1), (r == 2, L2), (r == 3, L3)
    )
    p1 = pick(
        jnp.where(even, SWAP, column), (r == 0, SWAP), (r == 1, LOW), (r == 2, L1), (r == 3, L2)
    )
    high = [
        HIGH,
        pick(U1, (r == n - 1, LOW)),
        pick(U2, (r == n - 2, EXTRA), (r == n - 1, L1)),
        pick(U3, (r == n - 2, LOW), (r == n - 1, L2)),
    ]
    return [p0, p1, LOW, L1, L2, L3], [p0, p1] + high


def attend_kernel(
    n, nbuf, heads, group, rank_ref, blocks_ref, len_ref, q_ref, g_ref, bias_ref, *refs
):
    bufs = refs[:nbuf]
    dq_ref, dbias_ref, own_ref = refs[nbuf : nbuf + 3]
    outs = refs[nbuf + 3 : nbuf + 3 + nbuf - 2]
    kv, acc, probs_buf, ds_buf, q_buf, g_buf, s_buf, dp_buf = refs[nbuf + 3 + nbuf - 2 :]
    t, k = pl.program_id(0), pl.program_id(1)
    r = rank_ref[0]
    scale = HEAD ** (-0.5)
    factor = scale * math.log2(math.e)
    width = 2 * BLOCK
    pairs = group // 2
    nt = (((1,), (1,)), ((), ()))
    part = [slice(c * BLOCK, (c + 1) * BLOCK) for c in range(CAND)]
    places = slots(r, n)

    @pl.when(k == 0)
    def _():
        for i in range(nbuf):
            kv[i] = bufs[i][0]

    acc[...] = jnp.zeros_like(acc)
    key_pos = lax.broadcasted_iota(jnp.int32, (BLOCK, width), 0)
    query_pos = lax.broadcasted_iota(jnp.int32, (BLOCK, width), 1) % BLOCK
    causal = key_pos <= query_pos

    def fold(op, x):
        return op(x.reshape(BLOCK // 8, 8, width), axis=0)

    keys, keys_t, vals, oks, lives = [], [], [], [], []
    for half in range(2):
        block = 2 * n - 1 - r if half else r
        base = (t * 2 * n + block) * CAND
        ok = []
        for c in range(CAND):
            listed = blocks_ref[base + c] >= 0
            if c < PROMPT:
                listed = listed & (c < block - WINDOW)
            ok.append(listed)
        oks.append(ok)
        lives.append(block * BLOCK + query_pos[:1] < len_ref[t])
        keys.append(jnp.concatenate([kv[s, k] for s in places[half]], axis=0))
        vals.append(jnp.concatenate([kv[s, heads + k] for s in places[half]], axis=0))
        keys_t.append(keys[half].T)

    def load(task):
        half, pair = divmod(task, pairs)
        for g in range(2 * pair, 2 * pair + 2):
            cols = slice(g * HEAD, (g + 1) * HEAD)
            rows = slice(g * BLOCK, (g + 1) * BLOCK)
            here = slice(half * BLOCK, (half + 1) * BLOCK)
            query = q_ref[0, here, cols].astype(jnp.float32) + bias_ref[:, cols]
            q_buf[half, rows] = query.astype(jnp.bfloat16)
            g_buf[half, rows] = g_ref[0, here, cols]

    def products(task):
        half, pair = divmod(task, pairs)
        rows = slice(pair * width, (pair + 1) * width)
        s_buf[task % 2] = lax.dot_general(
            keys[half], q_buf[half, rows], nt, preferred_element_type=jnp.float32
        )
        dp_buf[task % 2] = lax.dot_general(
            vals[half], g_buf[half, rows], nt, preferred_element_type=jnp.float32
        )

    def softmax(task):
        half, pair = divmod(task, pairs)
        span = slice(pair * width, (pair + 1) * width)
        slot = task % 2
        ok = oks[half]
        top = None
        for c in range(CAND):
            x = s_buf[slot, part[c]]
            if c == PROMPT:
                x = jnp.where(causal, x, -1e30)
            x = fold(jnp.max, x)
            if c != PROMPT:
                x = jnp.where(ok[c], x, -1e30)
            top = x if top is None else jnp.maximum(top, x)
        top = jnp.max(top, axis=0, keepdims=True) * factor
        total = jnp.zeros((8, width), jnp.float32)
        for c in range(CAND):
            x = s_buf[slot, part[c]]
            if c == PROMPT:
                e = jnp.exp2(jnp.where(causal, x, -1e30) * factor - top)
            else:
                e = jnp.exp2(x * factor - jnp.where(ok[c], top, 1e30))
            s_buf[slot, part[c]] = e
            total = total + fold(jnp.sum, e)
        total = jnp.sum(total, axis=0, keepdims=True)
        inverse = jnp.where(lives[half], 1.0 / total, 0.0)
        row_dot = jnp.zeros((8, width), jnp.float32)
        for c in range(CAND):
            low = (s_buf[slot, part[c]] * inverse).astype(jnp.bfloat16)
            probs_buf[half, part[c], span] = low
            row_dot = row_dot + fold(jnp.sum, low.astype(jnp.float32) * dp_buf[slot, part[c]])
        row_dot = jnp.sum(row_dot, axis=0, keepdims=True)
        for c in range(CAND):
            probs = s_buf[slot, part[c]] * inverse
            ds_buf[half, part[c], span] = (probs * (dp_buf[slot, part[c]] - row_dot)).astype(
                jnp.bfloat16
            )

    def query_grad(task):
        half, pair = divmod(task, pairs)
        span = slice(pair * width, (pair + 1) * width)
        here = slice(half * BLOCK, (half + 1) * BLOCK)
        dq = scale * jnp.dot(
            keys_t[half], ds_buf[half, :, span], preferred_element_type=jnp.float32
        )
        for i in range(2):
            cols = slice((2 * pair + i) * HEAD, (2 * pair + i + 1) * HEAD)
            dq_head = dq[:, i * BLOCK : (i + 1) * BLOCK].T
            dq_ref[0, here, cols] = dq_head.astype(jnp.bfloat16)
            row = jnp.sum(dq_head, axis=0, keepdims=True)
            if half == 0:
                dbias_ref[:, cols] = jnp.where(t == 0, 0.0, dbias_ref[:, cols]) + row
            else:
                dbias_ref[:, cols] += row

    def key_grad(task, count):
        half, pair = divmod(task, pairs)
        span = slice((pair - count + 1) * width, (pair + 1) * width)
        dk = scale * jnp.dot(
            ds_buf[half, :, span], q_buf[half, span], preferred_element_type=jnp.float32
        )
        dv = jnp.dot(
            probs_buf[half, :, span], g_buf[half, span], preferred_element_type=jnp.float32
        )
        for c in range(CAND):
            acc[places[half][c], 0] += dk[part[c]]
            acc[places[half][c], 1] += dv[part[c]]

    tasks = 2 * pairs
    load(0)
    products(0)
    for task in range(tasks):
        if task + 1 < tasks:
            load(task + 1)
            products(task + 1)
        softmax(task)
        query_grad(task)
        if task % pairs == pairs - 1:
            key_grad(task, pairs)

    for i in range(2):
        own_ref[0, i, :, 0] = acc[i]
    for i, out in enumerate(outs):
        out[0, :, 0] = acc[i + 2].astype(out.dtype)


def attend(n, heads, group, rank, blocks, lens, query_in, grad_out, bias, bufs):
    traces = query_in.shape[0]
    nbuf = len(bufs)
    width = group * HEAD
    row_spec = pl.BlockSpec((1, 2 * BLOCK, width), lambda t, k, *_: (t, 0, k))
    bias_spec = pl.BlockSpec((1, width), lambda t, k, *_: (0, k))
    buf_spec = pl.BlockSpec((1, 2 * heads, BLOCK, HEAD), lambda t, k, *_: (t, 0, 0, 0))
    own_spec = pl.BlockSpec((1, 2, 2, 1, BLOCK, HEAD), lambda t, k, *_: (t, 0, 0, k, 0, 0))
    out_spec = pl.BlockSpec((1, 2, 1, BLOCK, HEAD), lambda t, k, *_: (t, 0, k, 0, 0))
    out_shape = [
        jax.ShapeDtypeStruct(query_in.shape, jnp.bfloat16),
        jax.ShapeDtypeStruct((1, heads * width), jnp.float32),
        jax.ShapeDtypeStruct((traces, 2, 2, heads, BLOCK, HEAD), jnp.float32),
    ] + [jax.ShapeDtypeStruct((traces, 2, heads, BLOCK, HEAD), jnp.bfloat16)] * (nbuf - 2)
    return pl.pallas_call(
        functools.partial(attend_kernel, n, nbuf, heads, group),
        out_shape=out_shape,
        grid_spec=pltpu.PrefetchScalarGridSpec(
            num_scalar_prefetch=3,
            grid=(traces, heads),
            in_specs=[row_spec, row_spec, bias_spec] + [buf_spec] * nbuf,
            out_specs=[row_spec, bias_spec, own_spec] + [out_spec] * (nbuf - 2),
            scratch_shapes=[
                pltpu.VMEM((nbuf, 2 * heads, BLOCK, HEAD), jnp.bfloat16),
                pltpu.VMEM((nbuf, 2, BLOCK, HEAD), jnp.float32),
                pltpu.VMEM((2, CAND * BLOCK, width), jnp.bfloat16),
                pltpu.VMEM((2, CAND * BLOCK, width), jnp.bfloat16),
                pltpu.VMEM((2, width, HEAD), jnp.bfloat16),
                pltpu.VMEM((2, width, HEAD), jnp.bfloat16),
                pltpu.VMEM((2, CAND * BLOCK, 2 * BLOCK), jnp.float32),
                pltpu.VMEM((2, CAND * BLOCK, 2 * BLOCK), jnp.float32),
            ],
        ),
        compiler_params=pltpu.CompilerParams(
            dimension_semantics=("arbitrary", "arbitrary"),
            vmem_limit_bytes=56 * 1024 * 1024,
        ),
        name="attend",
    )(rank, blocks, lens, query_in, grad_out, bias, *bufs)


def butterfly(value, axis):
    count = lax.axis_size(axis)
    stride = 1
    while stride < count:
        got = lax.ppermute(value, axis, [(s, s ^ stride) for s in range(count)])
        value = value + got
        stride *= 2
    return value


def body(query_in, key_in, value_rows_input, grad_out, query_bias, key_blocks, trace_len):
    n = lax.axis_size("ctx")
    assert n >= 8 and n & (n - 1) == 0
    r = lax.axis_index("ctx")
    traces, _, width_q = query_in.shape
    width_kv = key_in.shape[-1]
    heads = width_kv // HEAD
    group = width_q // width_kv
    up1, down1, up2, ring2, down2, extra, swap, relay = plan(n)

    halves = jnp.concatenate([key_in, value_rows_input], axis=-1).reshape(
        traces, 2, BLOCK, 2 * heads, HEAD
    )
    low = halves[:, 0].transpose(0, 2, 1, 3)
    high = halves[:, 1].transpose(0, 2, 1, 3)
    in_l1 = send(low, up1)
    in_u1 = send(high, down1)
    in_l2 = send(low, up2)
    in_u2 = send(jnp.where(r < 2, low, high), ring2)
    in_ex = send(low, extra)
    column = jnp.where(r < 2, low, jnp.where(r < 6, in_ex, in_u2))
    bufs_relay = []
    for pairs in relay:
        got = send(column, pairs)
        targets = functools.reduce(jnp.logical_or, [r == b for _, b in pairs])
        column = jnp.where(targets, got, column)
    if relay:
        bufs_relay = [column]
    in_l3 = send(in_l1, up2)
    in_u3 = send(jnp.where(r == n - 1, low, in_u1), down2)
    in_sw = send(column, swap)
    bufs = [low, high, in_l1, in_u1, in_l2, in_u2, in_ex, in_l3, in_u3, in_sw] + bufs_relay

    dq, dbias, own, *outs = attend(
        n,
        heads,
        group,
        r.reshape(1).astype(jnp.int32),
        key_blocks.reshape(-1),
        trace_len,
        query_in,
        grad_out,
        query_bias.reshape(1, -1),
        bufs,
    )
    d_l1, d_u1, d_l2, d_u2, d_ex, d_l3, d_u3, d_sw = outs[:8]
    f32 = jnp.float32
    bf16 = jnp.bfloat16

    def gate(cond, value):
        return jnp.where(cond, value.astype(f32), 0.0)

    back_l3 = send_back(d_l3, up2)
    back_u3 = send_back(d_u3, down2)
    back_sw = send_back(d_sw, swap)
    back_l2 = send_back(d_l2, up2)
    d_l1 = (d_l1.astype(f32) + back_l3.astype(f32)).astype(bf16)
    d_u1 = (d_u1.astype(f32) + gate(r != n - 1, back_u3)).astype(bf16)
    back_l1 = send_back(d_l1, up1)
    back_u1 = send_back(d_u1, down1)
    if relay:
        d_rl = outs[8].astype(f32) + gate((r >= 6) & (r < n - 2), back_sw)
        d_ex = d_ex.astype(f32) + gate((r >= 4) & (r < 6), back_sw)
        d_u2 = d_u2.astype(f32) + gate(r >= n - 2, back_sw)
        low_extra = jnp.zeros_like(d_rl)
        for pairs in reversed(relay):
            is_from = functools.reduce(jnp.logical_or, [r == b for _, b in pairs])
            got = send_back(jnp.where(is_from, d_rl, 0.0).astype(bf16), pairs).astype(f32)
            low_extra = low_extra + gate(r < 2, got)
            d_ex = d_ex + gate((r >= 4) & (r < 6), got)
            d_u2 = d_u2 + gate(r >= n - 2, got)
            d_rl = d_rl + gate((r >= 6) & (r < n - 2), got)
        d_ex = d_ex.astype(bf16)
        d_u2 = d_u2.astype(bf16)
    else:
        d_ex = (d_ex.astype(f32) + gate((r >= 4) & (r < 6), back_sw)).astype(bf16)
        d_u2 = (d_u2.astype(f32) + gate(r >= n - 2, back_sw)).astype(bf16)
    back_ex = send_back(d_ex, extra)
    back_u2 = send_back(d_u2, ring2)

    low_grad = own[:, 0] + back_l1.astype(f32) + back_l2.astype(f32) + back_ex.astype(f32)
    low_grad = low_grad + gate(r < 2, back_u2) + gate(r == n - 1, back_u3) + gate(r == 1, back_sw)
    if relay:
        low_grad = low_grad + low_extra
    high_grad = own[:, 1] + back_u1.astype(f32) + gate(r >= 2, back_u2)
    both = jnp.stack([low_grad, high_grad], axis=1).astype(bf16)
    both = both.transpose(0, 1, 2, 4, 3, 5)
    grad_key = both[:, :, 0].reshape(traces, 2 * BLOCK, width_kv)
    grad_value = both[:, :, 1].reshape(traces, 2 * BLOCK, width_kv)
    bias_total = butterfly(butterfly(dbias.reshape(-1), "dp"), "ctx")
    rows = traces * lax.axis_size("dp") * 2 * BLOCK * n
    return dq, grad_key, grad_value, bias_total / math.sqrt(rows)


def solution(mesh):
    return jax.shard_map(
        body,
        mesh=mesh,
        in_specs=(
            P("dp", "ctx", None),
            P("dp", "ctx", None),
            P("dp", "ctx", None),
            P("dp", "ctx", None),
            P(),
            P("dp", None, None),
            P("dp"),
        ),
        out_specs=(P("dp", "ctx", None), P("dp", "ctx", None), P("dp", "ctx", None), P()),
        check_vma=False,
    )
```

```python
import functools
import math

import jax
import jax.numpy as jnp
from jax import lax
from jax.experimental import pallas as pl
from jax.experimental.pallas import tpu as pltpu

from jax.sharding import PartitionSpec as P


HEAD = 128
BLOCK = 128
PROMPT = 2
WINDOW = 3
CAND = PROMPT + WINDOW + 1

LOW, HIGH, A2, A3, B2, B3, C1, D1, NEAR, FAR, SWAP, RELAY = range(12)


def relay_rounds(n):
    known = [0, 2, n // 2 - 1]
    missing = list(range(3, n // 2 - 1))
    rounds = []
    while missing:
        pairs = list(zip(known, missing))
        rounds.append(pairs)
        known = known + [b for _, b in pairs]
        missing = missing[len(pairs) :]
    return rounds


def both_ways(pairs):
    return pairs + [(b, a) for a, b in pairs]


def plan(n):
    exchange = {
        "a": both_ways([(s, s + 2) for s in range(n - 2) if s & 2 == 0]),
        "b": both_ways([(s, s + 2) for s in range(n - 2) if s & 2]),
        "c": both_ways([(s, s + 1) for s in range(0, n, 2)]),
        "d": both_ways([(s, s + 1) for s in range(1, n - 1, 2)]),
        "near": [(0, 4), (1, 5), (n - 1, n - 2)],
        "far": [(0, n - 2), (1, n - 1)],
        "swap": [(1, 0)] + [(s, s ^ 1) for s in range(4, n)],
    }
    relay = [
        [(2 * a + x, 2 * b + x) for a, b in pairs for x in range(2)] for pairs in relay_rounds(n)
    ]
    return exchange, relay


def send(value, pairs):
    return lax.ppermute(value, "ctx", pairs)


def send_back(value, pairs):
    return lax.ppermute(value, "ctx", [(b, a) for a, b in pairs])


def slots(r, n):
    def pick(default, *cases):
        out = default
        for cond, value in reversed(cases):
            out = jnp.where(cond, value, out)
        return out

    even = r % 2 == 0
    upper = r & 2 != 0
    l1, u1 = jnp.where(even, D1, C1), jnp.where(even, C1, D1)
    l2, u2 = jnp.where(upper, A2, B2), jnp.where(upper, B2, A2)
    l3, u3 = jnp.where(upper, A3, B3), jnp.where(upper, B3, A3)
    column = pick(RELAY, (r < 6, NEAR), (r >= n - 2, FAR))
    p0 = pick(
        jnp.where(even, column, SWAP), (r == 0, LOW), (r == 1, l1), (r == 2, l2), (r == 3, l3)
    )
    p1 = pick(
        jnp.where(even, SWAP, column), (r == 0, SWAP), (r == 1, LOW), (r == 2, l1), (r == 3, l2)
    )
    high = [
        HIGH,
        pick(u1, (r == n - 1, LOW)),
        pick(u2, (r == n - 2, NEAR), (r == n - 1, l1)),
        pick(u3, (r == n - 2, LOW), (r == n - 1, l2)),
    ]
    return [p0, p1, LOW, l1, l2, l3], [p0, p1] + high


def attend_kernel(
    n, nbuf, heads, group, rank_ref, blocks_ref, len_ref, q_ref, g_ref, bias_ref, *refs
):
    bufs = refs[:nbuf]
    dq_ref, dbias_ref, own_ref = refs[nbuf : nbuf + 3]
    outs = refs[nbuf + 3 : nbuf + 3 + nbuf - 2]
    kv, acc, probs_buf, ds_buf, q_buf, g_buf, s_buf, dp_buf = refs[nbuf + 3 + nbuf - 2 :]
    t, k = pl.program_id(0), pl.program_id(1)
    r = rank_ref[0]
    scale = HEAD ** (-0.5)
    factor = scale * math.log2(math.e)
    width = 2 * BLOCK
    pairs = group // 2
    nt = (((1,), (1,)), ((), ()))
    part = [slice(c * BLOCK, (c + 1) * BLOCK) for c in range(CAND)]
    places = slots(r, n)

    @pl.when(k == 0)
    def _():
        for i in range(2):
            kv[i] = bufs[i][0]
            for j in range(2):
                kv[A2 + 2 * i + j] = bufs[2 + i][0, j]
        for i in range(4, nbuf):
            kv[i + 2] = bufs[i][0]

    acc[...] = jnp.zeros_like(acc)
    key_pos = lax.broadcasted_iota(jnp.int32, (BLOCK, width), 0)
    query_pos = lax.broadcasted_iota(jnp.int32, (BLOCK, width), 1) % BLOCK
    causal = key_pos <= query_pos

    def fold(op, x):
        return op(x.reshape(BLOCK // 8, 8, width), axis=0)

    keys, keys_t, vals, oks, lives = [], [], [], [], []
    for half in range(2):
        block = 2 * n - 1 - r if half else r
        base = (t * 2 * n + block) * CAND
        ok = []
        for c in range(CAND):
            listed = blocks_ref[base + c] >= 0
            if c < PROMPT:
                listed = listed & (c < block - WINDOW)
            ok.append(listed)
        oks.append(ok)
        lives.append(block * BLOCK + query_pos[:1] < len_ref[t])
        keys.append(jnp.concatenate([kv[s, k] for s in places[half]], axis=0))
        vals.append(jnp.concatenate([kv[s, heads + k] for s in places[half]], axis=0))
        keys_t.append(keys[half].T)

    def load(task):
        half, pair = divmod(task, pairs)
        for g in range(2 * pair, 2 * pair + 2):
            cols = slice(g * HEAD, (g + 1) * HEAD)
            rows = slice(g * BLOCK, (g + 1) * BLOCK)
            here = slice(half * BLOCK, (half + 1) * BLOCK)
            query = q_ref[0, here, cols].astype(jnp.float32) + bias_ref[:, cols]
            q_buf[half, rows] = query.astype(jnp.bfloat16)
            g_buf[half, rows] = g_ref[0, here, cols]

    def products(task):
        half, pair = divmod(task, pairs)
        rows = slice(pair * width, (pair + 1) * width)
        s_buf[task % 2] = lax.dot_general(
            keys[half], q_buf[half, rows], nt, preferred_element_type=jnp.float32
        )
        dp_buf[task % 2] = lax.dot_general(
            vals[half], g_buf[half, rows], nt, preferred_element_type=jnp.float32
        )

    def softmax(task):
        half, pair = divmod(task, pairs)
        span = slice(pair * width, (pair + 1) * width)
        slot = task % 2
        ok = oks[half]
        top = None
        for c in range(CAND):
            x = s_buf[slot, part[c]]
            if c == PROMPT:
                x = jnp.where(causal, x, -1e30)
            x = fold(jnp.max, x)
            if c != PROMPT:
                x = jnp.where(ok[c], x, -1e30)
            top = x if top is None else jnp.maximum(top, x)
        top = jnp.max(top, axis=0, keepdims=True) * factor
        total = jnp.zeros((8, width), jnp.float32)
        for c in range(CAND):
            x = s_buf[slot, part[c]]
            if c == PROMPT:
                e = jnp.exp2(jnp.where(causal, x, -1e30) * factor - top)
            else:
                e = jnp.exp2(x * factor - jnp.where(ok[c], top, 1e30))
            s_buf[slot, part[c]] = e
            total = total + fold(jnp.sum, e)
        total = jnp.sum(total, axis=0, keepdims=True)
        inverse = jnp.where(lives[half], 1.0 / total, 0.0)
        row_dot = jnp.zeros((8, width), jnp.float32)
        for c in range(CAND):
            low = (s_buf[slot, part[c]] * inverse).astype(jnp.bfloat16)
            probs_buf[half, part[c], span] = low
            row_dot = row_dot + fold(jnp.sum, low.astype(jnp.float32) * dp_buf[slot, part[c]])
        row_dot = jnp.sum(row_dot, axis=0, keepdims=True)
        for c in range(CAND):
            probs = s_buf[slot, part[c]] * inverse
            ds_buf[half, part[c], span] = (probs * (dp_buf[slot, part[c]] - row_dot)).astype(
                jnp.bfloat16
            )

    def query_grad(task):
        half, pair = divmod(task, pairs)
        span = slice(pair * width, (pair + 1) * width)
        here = slice(half * BLOCK, (half + 1) * BLOCK)
        dq = scale * jnp.dot(
            keys_t[half], ds_buf[half, :, span], preferred_element_type=jnp.float32
        )
        for i in range(2):
            cols = slice((2 * pair + i) * HEAD, (2 * pair + i + 1) * HEAD)
            dq_head = dq[:, i * BLOCK : (i + 1) * BLOCK].T
            dq_ref[0, here, cols] = dq_head.astype(jnp.bfloat16)
            row = jnp.sum(dq_head, axis=0, keepdims=True)
            if half == 0:
                dbias_ref[:, cols] = jnp.where(t == 0, 0.0, dbias_ref[:, cols]) + row
            else:
                dbias_ref[:, cols] += row

    def key_grad(task, count):
        half, pair = divmod(task, pairs)
        span = slice((pair - count + 1) * width, (pair + 1) * width)
        dk = scale * jnp.dot(
            ds_buf[half, :, span], q_buf[half, span], preferred_element_type=jnp.float32
        )
        dv = jnp.dot(
            probs_buf[half, :, span], g_buf[half, span], preferred_element_type=jnp.float32
        )
        for c in range(CAND):
            acc[places[half][c], 0] += dk[part[c]]
            acc[places[half][c], 1] += dv[part[c]]

    tasks = 2 * pairs
    load(0)
    products(0)
    for task in range(tasks):
        if task + 1 < tasks:
            load(task + 1)
            products(task + 1)
        softmax(task)
        query_grad(task)
        if task % pairs == pairs - 1:
            key_grad(task, pairs)

    for i in range(2):
        own_ref[0, i, :, 0] = acc[i]
    for i in range(2):
        for j in range(2):
            outs[i][0, j, :, 0] = acc[A2 + 2 * i + j].astype(jnp.bfloat16)
    for i in range(2, nbuf - 2):
        outs[i][0, :, 0] = acc[i + 4].astype(jnp.bfloat16)


def attend(n, heads, group, rank, blocks, lens, query_in, grad_out, bias, bufs):
    traces = query_in.shape[0]
    nbuf = len(bufs)
    width = group * HEAD
    row_spec = pl.BlockSpec((1, 2 * BLOCK, width), lambda t, k, *_: (t, 0, k))
    bias_spec = pl.BlockSpec((1, width), lambda t, k, *_: (0, k))
    buf_spec = pl.BlockSpec((1, 2 * heads, BLOCK, HEAD), lambda t, k, *_: (t, 0, 0, 0))
    own_spec = pl.BlockSpec((1, 2, 2, 1, BLOCK, HEAD), lambda t, k, *_: (t, 0, 0, k, 0, 0))
    out_spec = pl.BlockSpec((1, 2, 1, BLOCK, HEAD), lambda t, k, *_: (t, 0, k, 0, 0))
    two_spec = pl.BlockSpec((1, 2, 2 * heads, BLOCK, HEAD), lambda t, k, *_: (t, 0, 0, 0, 0))
    two_out = pl.BlockSpec((1, 2, 2, 1, BLOCK, HEAD), lambda t, k, *_: (t, 0, 0, k, 0, 0))
    out_shape = [
        jax.ShapeDtypeStruct(query_in.shape, jnp.bfloat16),
        jax.ShapeDtypeStruct((1, heads * width), jnp.float32),
        jax.ShapeDtypeStruct((traces, 2, 2, heads, BLOCK, HEAD), jnp.float32),
    ]
    out_shape += [jax.ShapeDtypeStruct((traces, 2, 2, heads, BLOCK, HEAD), jnp.bfloat16)] * 2
    out_shape += [jax.ShapeDtypeStruct((traces, 2, heads, BLOCK, HEAD), jnp.bfloat16)] * (nbuf - 4)
    return pl.pallas_call(
        functools.partial(attend_kernel, n, nbuf, heads, group),
        out_shape=out_shape,
        grid_spec=pltpu.PrefetchScalarGridSpec(
            num_scalar_prefetch=3,
            grid=(traces, heads),
            in_specs=[row_spec, row_spec, bias_spec]
            + [buf_spec] * 2
            + [two_spec] * 2
            + [buf_spec] * (nbuf - 4),
            out_specs=[row_spec, bias_spec, own_spec]
            + [two_out] * 2
            + [out_spec] * (nbuf - 4),
            scratch_shapes=[
                pltpu.VMEM((nbuf + 2, 2 * heads, BLOCK, HEAD), jnp.bfloat16),
                pltpu.VMEM((nbuf + 2, 2, BLOCK, HEAD), jnp.float32),
                pltpu.VMEM((2, CAND * BLOCK, width), jnp.bfloat16),
                pltpu.VMEM((2, CAND * BLOCK, width), jnp.bfloat16),
                pltpu.VMEM((2, width, HEAD), jnp.bfloat16),
                pltpu.VMEM((2, width, HEAD), jnp.bfloat16),
                pltpu.VMEM((2, CAND * BLOCK, 2 * BLOCK), jnp.float32),
                pltpu.VMEM((2, CAND * BLOCK, 2 * BLOCK), jnp.float32),
            ],
        ),
        compiler_params=pltpu.CompilerParams(
            dimension_semantics=("arbitrary", "arbitrary"),
            vmem_limit_bytes=56 * 1024 * 1024,
        ),
        name="attend",
    )(rank, blocks, lens, query_in, grad_out, bias, *bufs)


def butterfly(value, axis):
    count = lax.axis_size(axis)
    stride = 1
    while stride < count:
        got = lax.ppermute(value, axis, [(s, s ^ stride) for s in range(count)])
        value = value + got
        stride *= 2
    return value


def body(query_in, key_in, value_rows_input, grad_out, query_bias, key_blocks, trace_len):
    n = lax.axis_size("ctx")
    assert n >= 8 and n & (n - 1) == 0
    r = lax.axis_index("ctx")
    traces, _, width_q = query_in.shape
    width_kv = key_in.shape[-1]
    heads = width_kv // HEAD
    group = width_q // width_kv
    exchange, relay = plan(n)
    even = r % 2 == 0
    upper = r & 2 != 0

    halves = jnp.concatenate([key_in, value_rows_input], axis=-1).reshape(
        traces, 2, BLOCK, 2 * heads, HEAD
    )
    low = halves[:, 0].transpose(0, 2, 1, 3)
    high = halves[:, 1].transpose(0, 2, 1, 3)
    low, high, msg_c, msg_d = lax.optimization_barrier(
        (low, high, jnp.where(even, low, high), jnp.where(even, high, low))
    )
    in_c = send(msg_c, exchange["c"])
    in_d = send(msg_d, exchange["d"])
    in_near = send(low, exchange["near"])
    in_far = send(low, exchange["far"])
    low_again = lax.optimization_barrier(low)
    column = jnp.where(r < 2, low_again, jnp.where(r < 6, in_near, in_far))
    bufs_relay = []
    for pairs in relay:
        got = send(column, pairs)
        targets = functools.reduce(jnp.logical_or, [r == b for _, b in pairs])
        column = jnp.where(targets, got, column)
    if relay:
        bufs_relay = [column]
    to_up = jnp.stack([low, jnp.where(even, in_d, in_c)], axis=1)
    to_down = jnp.stack([high, jnp.where(r == n - 1, low, jnp.where(even, in_c, in_d))], axis=1)
    msg_a, msg_b = lax.optimization_barrier(
        (jnp.where(upper, to_down, to_up), jnp.where(upper, to_up, to_down))
    )
    in_a = send(msg_a, exchange["a"])
    in_b = send(msg_b, exchange["b"])
    in_sw = send(column, exchange["swap"])
    bufs = [low, high, in_a, in_b, in_c, in_d, in_near, in_far, in_sw] + bufs_relay

    dq, dbias, own, *outs = attend(
        n,
        heads,
        group,
        r.reshape(1).astype(jnp.int32),
        key_blocks.reshape(-1),
        trace_len,
        query_in,
        grad_out,
        query_bias.reshape(1, -1),
        bufs,
    )
    d_a, d_b, d_c, d_d, d_near, d_far, d_sw = outs[:7]
    f32 = jnp.float32
    bf16 = jnp.bfloat16

    def gate(cond, value):
        return jnp.where(cond, value.astype(f32), 0.0)

    back_a = send_back(d_a, exchange["a"])
    back_b = send_back(d_b, exchange["b"])
    back_sw = send_back(d_sw, exchange["swap"])
    from_up = jnp.where(upper, back_b, back_a).astype(f32)
    from_down = jnp.where(upper, back_a, back_b).astype(f32)
    d_c = (d_c.astype(f32) + jnp.where(even, from_down[:, 1], from_up[:, 1])).astype(bf16)
    d_d = (d_d.astype(f32) + jnp.where(even, from_up[:, 1], from_down[:, 1])).astype(bf16)
    d_near = d_near.astype(f32) + gate((r >= 4) & (r < 6), back_sw)
    d_far = d_far.astype(f32) + gate(r >= n - 2, back_sw)
    low_extra = 0.0
    if relay:
        d_relay = outs[7].astype(f32) + gate((r >= 6) & (r < n - 2), back_sw)
        for pairs in reversed(relay):
            is_from = functools.reduce(jnp.logical_or, [r == b for _, b in pairs])
            got = send_back(jnp.where(is_from, d_relay, 0.0).astype(bf16), pairs)
            low_extra = low_extra + gate(r < 2, got)
            d_near = d_near + gate((r >= 4) & (r < 6), got)
            d_far = d_far + gate(r >= n - 2, got)
            d_relay = d_relay + gate((r >= 6) & (r < n - 2), got)
    back_c = send_back(d_c, exchange["c"])
    back_d = send_back(d_d, exchange["d"])
    back_near = send_back(d_near.astype(bf16), exchange["near"])
    back_far = send_back(d_far.astype(bf16), exchange["far"])

    low_grad = own[:, 0] + from_up[:, 0] + gate(r == n - 1, from_down[:, 1])
    low_grad = low_grad + gate(r == 1, back_sw) + low_extra
    low_grad = low_grad + jnp.where(even, back_c, back_d).astype(f32)
    low_grad = low_grad + back_near.astype(f32) + back_far.astype(f32)
    high_grad = own[:, 1] + from_down[:, 0] + jnp.where(even, back_d, back_c).astype(f32)
    both = jnp.stack([low_grad, high_grad], axis=1).astype(bf16)
    both = both.transpose(0, 1, 2, 4, 3, 5)
    grad_key = both[:, :, 0].reshape(traces, 2 * BLOCK, width_kv)
    grad_value = both[:, :, 1].reshape(traces, 2 * BLOCK, width_kv)
    bias_total = butterfly(butterfly(dbias.reshape(-1), "ctx"), "dp")
    rows = traces * lax.axis_size("dp") * 2 * BLOCK * n
    return dq, grad_key, grad_value, bias_total / math.sqrt(rows)


def solution(mesh):
    return jax.shard_map(
        body,
        mesh=mesh,
        in_specs=(
            P("dp", "ctx", None),
            P("dp", "ctx", None),
            P("dp", "ctx", None),
            P("dp", "ctx", None),
            P(),
            P("dp", None, None),
            P("dp"),
        ),
        out_specs=(P("dp", "ctx", None), P("dp", "ctx", None), P("dp", "ctx", None), P()),
        check_vma=False,
    )
```

```python
import functools
import math

import jax
import jax.numpy as jnp
from jax import lax
from jax.experimental import pallas as pl
from jax.experimental.pallas import tpu as pltpu

from jax.sharding import PartitionSpec as P


HEAD = 128
BLOCK = 128
PROMPT = 2
WINDOW = 3
CAND = PROMPT + WINDOW + 1

LOW, HIGH, A2, A3, B2, B3, C1, D1, NEAR, FAR, SWAP, RELAY = range(12)


def relay_rounds(n):
    known = [0, 2, n // 2 - 1]
    missing = list(range(3, n // 2 - 1))
    rounds = []
    while missing:
        pairs = list(zip(known, missing))
        rounds.append(pairs)
        known = known + [b for _, b in pairs]
        missing = missing[len(pairs) :]
    return rounds


def both_ways(pairs):
    return pairs + [(b, a) for a, b in pairs]


def plan(n):
    exchange = {
        "a": both_ways([(s, s + 2) for s in range(n - 2) if s & 2 == 0]),
        "b": both_ways([(s, s + 2) for s in range(n - 2) if s & 2]),
        "c": both_ways([(s, s + 1) for s in range(0, n, 2)]),
        "d": both_ways([(s, s + 1) for s in range(1, n - 1, 2)]),
        "near": [(0, 4), (1, 5), (n - 1, n - 2)],
        "far": [(0, n - 2), (1, n - 1)],
        "swap": [(1, 0)] + [(s, s ^ 1) for s in range(4, n)],
    }
    relay = [
        [(2 * a + x, 2 * b + x) for a, b in pairs for x in range(2)] for pairs in relay_rounds(n)
    ]
    return exchange, relay


def send(value, pairs):
    return lax.ppermute(value, "ctx", pairs)


def send_back(value, pairs):
    return lax.ppermute(value, "ctx", [(b, a) for a, b in pairs])


def slots(r, n):
    def pick(default, *cases):
        out = default
        for cond, value in reversed(cases):
            out = jnp.where(cond, value, out)
        return out

    even = r % 2 == 0
    upper = r & 2 != 0
    l1, u1 = jnp.where(even, D1, C1), jnp.where(even, C1, D1)
    l2, u2 = jnp.where(upper, A2, B2), jnp.where(upper, B2, A2)
    l3, u3 = jnp.where(upper, A3, B3), jnp.where(upper, B3, A3)
    column = pick(RELAY, (r < 6, NEAR), (r >= n - 2, FAR))
    p0 = pick(
        jnp.where(even, column, SWAP), (r == 0, LOW), (r == 1, l1), (r == 2, l2), (r == 3, l3)
    )
    p1 = pick(
        jnp.where(even, SWAP, column), (r == 0, SWAP), (r == 1, LOW), (r == 2, l1), (r == 3, l2)
    )
    high = [
        HIGH,
        pick(u1, (r == n - 1, LOW)),
        pick(u2, (r == n - 2, NEAR), (r == n - 1, l1)),
        pick(u3, (r == n - 2, LOW), (r == n - 1, l2)),
    ]
    return [p0, p1, LOW, l1, l2, l3], [p0, p1] + high


def attend_kernel(
    n, nbuf, heads, group, rank_ref, blocks_ref, len_ref, q_ref, g_ref, bias_ref, *refs
):
    bufs = refs[:nbuf]
    dq_ref, dbias_ref, own_ref = refs[nbuf : nbuf + 3]
    outs = refs[nbuf + 3 : nbuf + 3 + nbuf - 2]
    kv, acc, probs_buf, ds_buf, q_buf, g_buf, s_buf, dp_buf = refs[nbuf + 3 + nbuf - 2 :]
    t, k = pl.program_id(0), pl.program_id(1)
    r = rank_ref[0]
    scale = HEAD ** (-0.5)
    factor = scale * math.log2(math.e)
    width = 2 * BLOCK
    pairs = group // 2
    nt = (((1,), (1,)), ((), ()))
    part = [slice(c * BLOCK, (c + 1) * BLOCK) for c in range(CAND)]
    places = slots(r, n)

    @pl.when(k == 0)
    def _():
        for i in range(2):
            kv[i] = bufs[i][0]
            for j in range(2):
                kv[A2 + 2 * i + j] = bufs[2 + i][0, j]
        for i in range(4, nbuf):
            kv[i + 2] = bufs[i][0]

    acc[...] = jnp.zeros_like(acc)
    key_pos = lax.broadcasted_iota(jnp.int32, (BLOCK, width), 0)
    query_pos = lax.broadcasted_iota(jnp.int32, (BLOCK, width), 1) % BLOCK
    causal = key_pos <= query_pos

    def fold(op, x):
        return op(x.reshape(BLOCK // 8, 8, width), axis=0)

    keys, keys_t, vals, oks, lives = [], [], [], [], []
    for half in range(2):
        block = 2 * n - 1 - r if half else r
        base = (t * 2 * n + block) * CAND
        ok = []
        for c in range(CAND):
            listed = blocks_ref[base + c] >= 0
            if c < PROMPT:
                listed = listed & (c < block - WINDOW)
            ok.append(listed)
        oks.append(ok)
        lives.append(block * BLOCK + query_pos[:1] < len_ref[t])
        keys.append(jnp.concatenate([kv[s, k] for s in places[half]], axis=0))
        vals.append(jnp.concatenate([kv[s, heads + k] for s in places[half]], axis=0))
        keys_t.append(keys[half].T)

    def load(task):
        half, pair = divmod(task, pairs)
        for g in range(2 * pair, 2 * pair + 2):
            cols = slice(g * HEAD, (g + 1) * HEAD)
            rows = slice(g * BLOCK, (g + 1) * BLOCK)
            here = slice(half * BLOCK, (half + 1) * BLOCK)
            query = q_ref[0, here, cols].astype(jnp.float32) + bias_ref[:, cols]
            q_buf[half, rows] = query.astype(jnp.bfloat16)
            g_buf[half, rows] = g_ref[0, here, cols]

    def products(task):
        half, pair = divmod(task, pairs)
        rows = slice(pair * width, (pair + 1) * width)
        s_buf[task % 2] = lax.dot_general(
            keys[half], q_buf[half, rows], nt, preferred_element_type=jnp.float32
        )
        dp_buf[task % 2] = lax.dot_general(
            vals[half], g_buf[half, rows], nt, preferred_element_type=jnp.float32
        )

    def softmax(task):
        half, pair = divmod(task, pairs)
        span = slice(pair * width, (pair + 1) * width)
        slot = task % 2
        ok = oks[half]
        top = None
        for c in range(CAND):
            x = s_buf[slot, part[c]]
            if c == PROMPT:
                x = jnp.where(causal, x, -1e30)
            x = fold(jnp.max, x)
            if c != PROMPT:
                x = jnp.where(ok[c], x, -1e30)
            top = x if top is None else jnp.maximum(top, x)
        top = jnp.max(top, axis=0, keepdims=True) * factor
        total = jnp.zeros((8, width), jnp.float32)
        for c in range(CAND):
            x = s_buf[slot, part[c]]
            if c == PROMPT:
                e = jnp.exp2(jnp.where(causal, x, -1e30) * factor - top)
            else:
                e = jnp.exp2(x * factor - jnp.where(ok[c], top, 1e30))
            s_buf[slot, part[c]] = e
            total = total + fold(jnp.sum, e)
        total = jnp.sum(total, axis=0, keepdims=True)
        inverse = jnp.where(lives[half], 1.0 / total, 0.0)
        row_dot = jnp.zeros((8, width), jnp.float32)
        for c in range(CAND):
            low = (s_buf[slot, part[c]] * inverse).astype(jnp.bfloat16)
            probs_buf[half, part[c], span] = low
            row_dot = row_dot + fold(jnp.sum, low.astype(jnp.float32) * dp_buf[slot, part[c]])
        row_dot = jnp.sum(row_dot, axis=0, keepdims=True)
        for c in range(CAND):
            probs = s_buf[slot, part[c]] * inverse
            ds_buf[half, part[c], span] = (probs * (dp_buf[slot, part[c]] - row_dot)).astype(
                jnp.bfloat16
            )

    def query_grad(task):
        half, pair = divmod(task, pairs)
        span = slice(pair * width, (pair + 1) * width)
        here = slice(half * BLOCK, (half + 1) * BLOCK)
        dq = scale * jnp.dot(
            keys_t[half], ds_buf[half, :, span], preferred_element_type=jnp.float32
        )
        for i in range(2):
            cols = slice((2 * pair + i) * HEAD, (2 * pair + i + 1) * HEAD)
            dq_head = dq[:, i * BLOCK : (i + 1) * BLOCK].T
            dq_ref[0, here, cols] = dq_head.astype(jnp.bfloat16)
            row = jnp.sum(dq_head, axis=0, keepdims=True)
            if half == 0:
                dbias_ref[:, cols] = jnp.where(t == 0, 0.0, dbias_ref[:, cols]) + row
            else:
                dbias_ref[:, cols] += row

    def key_grad(task, count, which=(0, 1)):
        half, pair = divmod(task, pairs)
        span = slice((pair - count + 1) * width, (pair + 1) * width)
        for value in which:
            if value:
                grad = jnp.dot(
                    probs_buf[half, :, span], g_buf[half, span], preferred_element_type=jnp.float32
                )
            else:
                grad = scale * jnp.dot(
                    ds_buf[half, :, span], q_buf[half, span], preferred_element_type=jnp.float32
                )
            for c in range(CAND):
                acc[places[half][c], value] += grad[part[c]]

    tasks = 2 * pairs
    load(0)
    products(0)
    for task in range(tasks):
        if task + 1 < tasks:
            load(task + 1)
            products(task + 1)
        if task > 0:
            query_grad(task - 1)
            if task % 2 == 0:
                key_grad(task - 1, 2, (0,))
            elif task > 1:
                key_grad(task - 2, 2, (1,))
        softmax(task)
    query_grad(tasks - 1)
    key_grad(tasks - 1, 2)

    for i in range(2):
        own_ref[0, i, :, 0] = acc[i]
    for i in range(2):
        for j in range(2):
            outs[i][0, j, :, 0] = acc[A2 + 2 * i + j].astype(jnp.bfloat16)
    for i in range(2, nbuf - 2):
        outs[i][0, :, 0] = acc[i + 4].astype(jnp.bfloat16)


def attend(n, heads, group, rank, blocks, lens, query_in, grad_out, bias, bufs):
    traces = query_in.shape[0]
    nbuf = len(bufs)
    width = group * HEAD
    row_spec = pl.BlockSpec((1, 2 * BLOCK, width), lambda t, k, *_: (t, 0, k))
    bias_spec = pl.BlockSpec((1, width), lambda t, k, *_: (0, k))
    buf_spec = pl.BlockSpec((1, 2 * heads, BLOCK, HEAD), lambda t, k, *_: (t, 0, 0, 0))
    own_spec = pl.BlockSpec((1, 2, 2, 1, BLOCK, HEAD), lambda t, k, *_: (t, 0, 0, k, 0, 0))
    out_spec = pl.BlockSpec((1, 2, 1, BLOCK, HEAD), lambda t, k, *_: (t, 0, k, 0, 0))
    two_spec = pl.BlockSpec((1, 2, 2 * heads, BLOCK, HEAD), lambda t, k, *_: (t, 0, 0, 0, 0))
    two_out = pl.BlockSpec((1, 2, 2, 1, BLOCK, HEAD), lambda t, k, *_: (t, 0, 0, k, 0, 0))
    out_shape = [
        jax.ShapeDtypeStruct(query_in.shape, jnp.bfloat16),
        jax.ShapeDtypeStruct((1, heads * width), jnp.float32),
        jax.ShapeDtypeStruct((traces, 2, 2, heads, BLOCK, HEAD), jnp.float32),
    ]
    out_shape += [jax.ShapeDtypeStruct((traces, 2, 2, heads, BLOCK, HEAD), jnp.bfloat16)] * 2
    out_shape += [jax.ShapeDtypeStruct((traces, 2, heads, BLOCK, HEAD), jnp.bfloat16)] * (nbuf - 4)
    return pl.pallas_call(
        functools.partial(attend_kernel, n, nbuf, heads, group),
        out_shape=out_shape,
        grid_spec=pltpu.PrefetchScalarGridSpec(
            num_scalar_prefetch=3,
            grid=(traces, heads),
            in_specs=[row_spec, row_spec, bias_spec]
            + [buf_spec] * 2
            + [two_spec] * 2
            + [buf_spec] * (nbuf - 4),
            out_specs=[row_spec, bias_spec, own_spec]
            + [two_out] * 2
            + [out_spec] * (nbuf - 4),
            scratch_shapes=[
                pltpu.VMEM((nbuf + 2, 2 * heads, BLOCK, HEAD), jnp.bfloat16),
                pltpu.VMEM((nbuf + 2, 2, BLOCK, HEAD), jnp.float32),
                pltpu.VMEM((2, CAND * BLOCK, width), jnp.bfloat16),
                pltpu.VMEM((2, CAND * BLOCK, width), jnp.bfloat16),
                pltpu.VMEM((2, width, HEAD), jnp.bfloat16),
                pltpu.VMEM((2, width, HEAD), jnp.bfloat16),
                pltpu.VMEM((2, CAND * BLOCK, 2 * BLOCK), jnp.float32),
                pltpu.VMEM((2, CAND * BLOCK, 2 * BLOCK), jnp.float32),
            ],
        ),
        compiler_params=pltpu.CompilerParams(
            dimension_semantics=("arbitrary", "arbitrary"),
            vmem_limit_bytes=56 * 1024 * 1024,
        ),
        name="attend",
    )(rank, blocks, lens, query_in, grad_out, bias, *bufs)


def swapped(value, axis, stride):
    pairs = [(s, s ^ stride) for s in range(lax.axis_size(axis))]
    return lax.ppermute(value, axis, pairs)


def butterfly(value, axis, stride=1, stop=None):
    stop = lax.axis_size(axis) if stop is None else stop
    while stride < stop:
        value = value + swapped(value, axis, stride)
        stride *= 2
    return value


def quad(value, axis, stride):
    first, second, third = (swapped(value, axis, i * stride) for i in (1, 2, 3))
    return (value + first) + (second + third)


def body(query_in, key_in, value_rows_input, grad_out, query_bias, key_blocks, trace_len):
    n = lax.axis_size("ctx")
    assert n >= 8 and n & (n - 1) == 0
    r = lax.axis_index("ctx")
    traces, _, width_q = query_in.shape
    width_kv = key_in.shape[-1]
    heads = width_kv // HEAD
    group = width_q // width_kv
    exchange, relay = plan(n)
    even = r % 2 == 0
    upper = r & 2 != 0

    halves = jnp.concatenate([key_in, value_rows_input], axis=-1).reshape(
        traces, 2, BLOCK, 2 * heads, HEAD
    )
    low = halves[:, 0].transpose(0, 2, 1, 3)
    high = halves[:, 1].transpose(0, 2, 1, 3)
    low, high, msg_c, msg_d = lax.optimization_barrier(
        (low, high, jnp.where(even, low, high), jnp.where(even, high, low))
    )
    in_c = send(msg_c, exchange["c"])
    in_d = send(msg_d, exchange["d"])
    in_near = send(low, exchange["near"])
    in_far = send(low, exchange["far"])
    low_again = lax.optimization_barrier(low)
    column = jnp.where(r < 2, low_again, jnp.where(r < 6, in_near, in_far))
    bufs_relay = []
    for pairs in relay:
        got = send(column, pairs)
        targets = functools.reduce(jnp.logical_or, [r == b for _, b in pairs])
        column = jnp.where(targets, got, column)
    if relay:
        bufs_relay = [column]
    to_up = jnp.stack([low, jnp.where(even, in_d, in_c)], axis=1)
    to_down = jnp.stack([high, jnp.where(r == n - 1, low, jnp.where(even, in_c, in_d))], axis=1)
    msg_a, msg_b = lax.optimization_barrier(
        (jnp.where(upper, to_down, to_up), jnp.where(upper, to_up, to_down))
    )
    in_a = send(msg_a, exchange["a"])
    in_b = send(msg_b, exchange["b"])
    in_sw = send(column, exchange["swap"])
    bufs = [low, high, in_a, in_b, in_c, in_d, in_near, in_far, in_sw] + bufs_relay

    dq, dbias, own, *outs = attend(
        n,
        heads,
        group,
        r.reshape(1).astype(jnp.int32),
        key_blocks.reshape(-1),
        trace_len,
        query_in,
        grad_out,
        query_bias.reshape(1, -1),
        bufs,
    )
    d_a, d_b, d_c, d_d, d_near, d_far, d_sw = outs[:7]
    f32 = jnp.float32
    bf16 = jnp.bfloat16

    def gate(cond, value):
        return jnp.where(cond, value.astype(f32), 0.0)

    back_a = send_back(d_a, exchange["a"])
    back_b = send_back(d_b, exchange["b"])
    back_sw = send_back(d_sw, exchange["swap"])
    from_up = jnp.where(upper, back_b, back_a).astype(f32)
    from_down = jnp.where(upper, back_a, back_b).astype(f32)
    d_c = (d_c.astype(f32) + jnp.where(even, from_down[:, 1], from_up[:, 1])).astype(bf16)
    d_d = (d_d.astype(f32) + jnp.where(even, from_up[:, 1], from_down[:, 1])).astype(bf16)
    d_near = d_near.astype(f32) + gate((r >= 4) & (r < 6), back_sw)
    d_far = d_far.astype(f32) + gate(r >= n - 2, back_sw)
    low_extra = 0.0
    if relay:
        d_relay = outs[7].astype(f32) + gate((r >= 6) & (r < n - 2), back_sw)
        for pairs in reversed(relay):
            is_from = functools.reduce(jnp.logical_or, [r == b for _, b in pairs])
            got = send_back(jnp.where(is_from, d_relay, 0.0).astype(bf16), pairs)
            low_extra = low_extra + gate(r < 2, got)
            d_near = d_near + gate((r >= 4) & (r < 6), got)
            d_far = d_far + gate(r >= n - 2, got)
            d_relay = d_relay + gate((r >= 6) & (r < n - 2), got)
    back_c = send_back(d_c, exchange["c"])
    back_d = send_back(d_d, exchange["d"])
    back_near = send_back(d_near.astype(bf16), exchange["near"])
    back_far = send_back(d_far.astype(bf16), exchange["far"])

    low_grad = own[:, 0] + from_up[:, 0] + gate(r == n - 1, from_down[:, 1])
    low_grad = low_grad + gate(r == 1, back_sw) + low_extra
    low_grad = low_grad + jnp.where(even, back_c, back_d).astype(f32)
    low_grad = low_grad + back_near.astype(f32) + back_far.astype(f32)
    high_grad = own[:, 1] + from_down[:, 0] + jnp.where(even, back_d, back_c).astype(f32)
    both = jnp.stack([low_grad, high_grad], axis=1).astype(bf16)
    grad_key, grad_value = (
        jnp.concatenate([both[:, :, i, h] for h in range(heads)], axis=-1).reshape(
            traces, 2 * BLOCK, width_kv
        )
        for i in range(2)
    )
    bias_total = butterfly(butterfly(quad(butterfly(dbias.reshape(-1), "ctx", 1, 2), "ctx", 2), "ctx", 8), "dp")
    rows = traces * lax.axis_size("dp") * 2 * BLOCK * n
    return dq, grad_key, grad_value, bias_total / math.sqrt(rows)


def solution(mesh):
    return jax.shard_map(
        body,
        mesh=mesh,
        in_specs=(
            P("dp", "ctx", None),
            P("dp", "ctx", None),
            P("dp", "ctx", None),
            P("dp", "ctx", None),
            P(),
            P("dp", None, None),
            P("dp"),
        ),
        out_specs=(P("dp", "ctx", None), P("dp", "ctx", None), P("dp", "ctx", None), P()),
        check_vma=False,
    )
```

```python
import functools
import math

import jax
import jax.numpy as jnp
from jax import lax
from jax.experimental import pallas as pl
from jax.experimental.pallas import tpu as pltpu

from jax.sharding import PartitionSpec as P


HEAD = 128
BLOCK = 128
PROMPT = 2
WINDOW = 3
CAND = PROMPT + WINDOW + 1

LOW, HIGH, A2, A3, B2, B3, C1, D1, NEAR, FAR, SWAP, RELAY = range(12)


def relay_rounds(n):
    known = [0, 2, n // 2 - 1]
    missing = list(range(3, n // 2 - 1))
    rounds = []
    while missing:
        pairs = list(zip(known, missing))
        rounds.append(pairs)
        known = known + [b for _, b in pairs]
        missing = missing[len(pairs) :]
    return rounds


def both_ways(pairs):
    return pairs + [(b, a) for a, b in pairs]


def plan(n):
    exchange = {
        "a": both_ways([(s, s + 2) for s in range(n - 2) if s & 2 == 0]),
        "b": both_ways([(s, s + 2) for s in range(n - 2) if s & 2]),
        "c": both_ways([(s, s + 1) for s in range(0, n, 2)]),
        "d": both_ways([(s, s + 1) for s in range(1, n - 1, 2)]),
        "near": [(0, 4), (1, 5), (n - 1, n - 2)],
        "far": [(0, n - 2), (1, n - 1)],
        "swap": [(1, 0)] + [(s, s ^ 1) for s in range(4, n)],
    }
    relay = [
        [(2 * a + x, 2 * b + x) for a, b in pairs for x in range(2)] for pairs in relay_rounds(n)
    ]
    return exchange, relay


def send(value, pairs):
    return lax.ppermute(value, "ctx", pairs)


def send_back(value, pairs):
    return lax.ppermute(value, "ctx", [(b, a) for a, b in pairs])


def slots(r, n):
    def pick(default, *cases):
        out = default
        for cond, value in reversed(cases):
            out = jnp.where(cond, value, out)
        return out

    even = r % 2 == 0
    upper = r & 2 != 0
    l1, u1 = jnp.where(even, D1, C1), jnp.where(even, C1, D1)
    l2, u2 = jnp.where(upper, A2, B2), jnp.where(upper, B2, A2)
    l3, u3 = jnp.where(upper, A3, B3), jnp.where(upper, B3, A3)
    column = pick(RELAY, (r < 6, NEAR), (r >= n - 2, FAR))
    p0 = pick(
        jnp.where(even, column, SWAP), (r == 0, LOW), (r == 1, l1), (r == 2, l2), (r == 3, l3)
    )
    p1 = pick(
        jnp.where(even, SWAP, column), (r == 0, SWAP), (r == 1, LOW), (r == 2, l1), (r == 3, l2)
    )
    high = [
        HIGH,
        pick(u1, (r == n - 1, LOW)),
        pick(u2, (r == n - 2, NEAR), (r == n - 1, l1)),
        pick(u3, (r == n - 2, LOW), (r == n - 1, l2)),
    ]
    return [p0, p1, LOW, l1, l2, l3], [p0, p1] + high


def attend_kernel(
    n, nbuf, heads, group, rank_ref, blocks_ref, len_ref, q_ref, g_ref, bias_ref, *refs
):
    bufs = refs[:nbuf]
    dq_ref, dbias_ref, own_ref = refs[nbuf : nbuf + 3]
    outs = refs[nbuf + 3 : nbuf + 3 + nbuf - 2]
    kv, acc, probs_buf, ds_buf, q_buf, g_buf, s_buf, dp_buf = refs[nbuf + 3 + nbuf - 2 :]
    t, k = pl.program_id(0), pl.program_id(1)
    r = rank_ref[0]
    scale = HEAD ** (-0.5)
    factor = scale * math.log2(math.e)
    width = 2 * BLOCK
    pairs = group // 2
    nt = (((1,), (1,)), ((), ()))
    part = [slice(c * BLOCK, (c + 1) * BLOCK) for c in range(CAND)]
    places = slots(r, n)

    @pl.when(k == 0)
    def _():
        for i in range(2):
            kv[i] = bufs[i][0]
            for j in range(2):
                kv[A2 + 2 * i + j] = bufs[2 + i][0, j]
        for i in range(4, nbuf):
            kv[i + 2] = bufs[i][0]

    acc[...] = jnp.zeros_like(acc)
    key_pos = lax.broadcasted_iota(jnp.int32, (BLOCK, width), 0)
    query_pos = lax.broadcasted_iota(jnp.int32, (BLOCK, width), 1) % BLOCK
    causal = key_pos <= query_pos

    def fold(op, x):
        return op(x.reshape(BLOCK // 8, 8, width), axis=0)

    keys, keys_t, vals, oks, lives = [], [], [], [], []
    for half in range(2):
        block = 2 * n - 1 - r if half else r
        base = (t * 2 * n + block) * CAND
        ok = []
        for c in range(CAND):
            listed = blocks_ref[base + c] >= 0
            if c < PROMPT:
                listed = listed & (c < block - WINDOW)
            ok.append(listed)
        oks.append(ok)
        lives.append(block * BLOCK + query_pos[:1] < len_ref[t])
        keys.append(jnp.concatenate([kv[s, k] for s in places[half]], axis=0))
        vals.append(jnp.concatenate([kv[s, heads + k] for s in places[half]], axis=0))
        keys_t.append(keys[half].T)

    def load(task):
        half, pair = divmod(task, pairs)
        for g in range(2 * pair, 2 * pair + 2):
            cols = slice(g * HEAD, (g + 1) * HEAD)
            rows = slice(g * BLOCK, (g + 1) * BLOCK)
            here = slice(half * BLOCK, (half + 1) * BLOCK)
            query = q_ref[0, here, cols].astype(jnp.float32) + bias_ref[:, cols]
            q_buf[half, rows] = query.astype(jnp.bfloat16)
            g_buf[half, rows] = g_ref[0, here, cols]

    def products(task):
        half, pair = divmod(task, pairs)
        rows = slice(pair * width, (pair + 1) * width)
        s_buf[task % 2] = lax.dot_general(
            keys[half], q_buf[half, rows], nt, preferred_element_type=jnp.float32
        )
        dp_buf[task % 2] = lax.dot_general(
            vals[half], g_buf[half, rows], nt, preferred_element_type=jnp.float32
        )

    def softmax(task):
        half, pair = divmod(task, pairs)
        span = slice(pair * width, (pair + 1) * width)
        slot = task % 2
        ok = oks[half]
        top = None
        for c in range(CAND):
            x = s_buf[slot, part[c]]
            if c == PROMPT:
                x = jnp.where(causal, x, -1e30)
            x = fold(jnp.max, x)
            if c != PROMPT:
                x = jnp.where(ok[c], x, -1e30)
            top = x if top is None else jnp.maximum(top, x)
        top = jnp.max(top, axis=0, keepdims=True) * factor
        total = jnp.zeros((8, width), jnp.float32)
        for c in range(CAND):
            x = s_buf[slot, part[c]]
            if c == PROMPT:
                e = jnp.exp2(jnp.where(causal, x, -1e30) * factor - top)
            else:
                e = jnp.exp2(x * factor - jnp.where(ok[c], top, 1e30))
            s_buf[slot, part[c]] = e
            total = total + fold(jnp.sum, e)
        total = jnp.sum(total, axis=0, keepdims=True)
        inverse = jnp.where(lives[half], 1.0 / total, 0.0)
        row_dot = jnp.zeros((8, width), jnp.float32)
        for c in range(CAND):
            low = (s_buf[slot, part[c]] * inverse).astype(jnp.bfloat16)
            probs_buf[half, part[c], span] = low
            row_dot = row_dot + fold(jnp.sum, low.astype(jnp.float32) * dp_buf[slot, part[c]])
        row_dot = jnp.sum(row_dot, axis=0, keepdims=True)
        for c in range(CAND):
            probs = s_buf[slot, part[c]] * inverse
            ds_buf[half, part[c], span] = (probs * (dp_buf[slot, part[c]] - row_dot)).astype(
                jnp.bfloat16
            )

    def query_grad(task):
        half, pair = divmod(task, pairs)
        span = slice(pair * width, (pair + 1) * width)
        here = slice(half * BLOCK, (half + 1) * BLOCK)
        dq = scale * jnp.dot(
            keys_t[half], ds_buf[half, :, span], preferred_element_type=jnp.float32
        )
        for i in range(2):
            cols = slice((2 * pair + i) * HEAD, (2 * pair + i + 1) * HEAD)
            dq_head = dq[:, i * BLOCK : (i + 1) * BLOCK].T
            dq_ref[0, here, cols] = dq_head.astype(jnp.bfloat16)
            row = jnp.sum(dq_head, axis=0, keepdims=True)
            if half == 0:
                dbias_ref[:, cols] = jnp.where(t == 0, 0.0, dbias_ref[:, cols]) + row
            else:
                dbias_ref[:, cols] += row

    def key_grad(task, count, which=(0, 1)):
        half, pair = divmod(task, pairs)
        span = slice((pair - count + 1) * width, (pair + 1) * width)
        for value in which:
            if value:
                grad = jnp.dot(
                    probs_buf[half, :, span], g_buf[half, span], preferred_element_type=jnp.float32
                )
            else:
                grad = scale * jnp.dot(
                    ds_buf[half, :, span], q_buf[half, span], preferred_element_type=jnp.float32
                )
            for c in range(CAND):
                acc[places[half][c], value] += grad[part[c]]

    tasks = 2 * pairs
    load(0)
    products(0)
    for task in range(tasks):
        if task + 1 < tasks:
            load(task + 1)
            products(task + 1)
        if task > 0:
            query_grad(task - 1)
            if task % 2 == 0:
                key_grad(task - 1, 2, (1,))
            elif task > 1:
                key_grad(task - 2, 2, (0,))
        softmax(task)
    query_grad(tasks - 1)
    key_grad(tasks - 1, 2)

    for i in range(2):
        own_ref[0, i, :, 0] = acc[i]
    for i in range(2):
        for j in range(2):
            outs[i][0, j, :, 0] = acc[A2 + 2 * i + j].astype(jnp.bfloat16)
    for i in range(2, nbuf - 2):
        outs[i][0, :, 0] = acc[i + 4].astype(jnp.bfloat16)


def attend(n, heads, group, rank, blocks, lens, query_in, grad_out, bias, bufs):
    traces = query_in.shape[0]
    nbuf = len(bufs)
    width = group * HEAD
    row_spec = pl.BlockSpec((1, 2 * BLOCK, width), lambda t, k, *_: (t, 0, k))
    bias_spec = pl.BlockSpec((1, width), lambda t, k, *_: (0, k))
    buf_spec = pl.BlockSpec((1, 2 * heads, BLOCK, HEAD), lambda t, k, *_: (t, 0, 0, 0))
    own_spec = pl.BlockSpec((1, 2, 2, 1, BLOCK, HEAD), lambda t, k, *_: (t, 0, 0, k, 0, 0))
    out_spec = pl.BlockSpec((1, 2, 1, BLOCK, HEAD), lambda t, k, *_: (t, 0, k, 0, 0))
    two_spec = pl.BlockSpec((1, 2, 2 * heads, BLOCK, HEAD), lambda t, k, *_: (t, 0, 0, 0, 0))
    two_out = pl.BlockSpec((1, 2, 2, 1, BLOCK, HEAD), lambda t, k, *_: (t, 0, 0, k, 0, 0))
    out_shape = [
        jax.ShapeDtypeStruct(query_in.shape, jnp.bfloat16),
        jax.ShapeDtypeStruct((1, heads * width), jnp.float32),
        jax.ShapeDtypeStruct((traces, 2, 2, heads, BLOCK, HEAD), jnp.float32),
    ]
    out_shape += [jax.ShapeDtypeStruct((traces, 2, 2, heads, BLOCK, HEAD), jnp.bfloat16)] * 2
    out_shape += [jax.ShapeDtypeStruct((traces, 2, heads, BLOCK, HEAD), jnp.bfloat16)] * (nbuf - 4)
    return pl.pallas_call(
        functools.partial(attend_kernel, n, nbuf, heads, group),
        out_shape=out_shape,
        grid_spec=pltpu.PrefetchScalarGridSpec(
            num_scalar_prefetch=3,
            grid=(traces, heads),
            in_specs=[row_spec, row_spec, bias_spec]
            + [buf_spec] * 2
            + [two_spec] * 2
            + [buf_spec] * (nbuf - 4),
            out_specs=[row_spec, bias_spec, own_spec]
            + [two_out] * 2
            + [out_spec] * (nbuf - 4),
            scratch_shapes=[
                pltpu.VMEM((nbuf + 2, 2 * heads, BLOCK, HEAD), jnp.bfloat16),
                pltpu.VMEM((nbuf + 2, 2, BLOCK, HEAD), jnp.float32),
                pltpu.VMEM((2, CAND * BLOCK, width), jnp.bfloat16),
                pltpu.VMEM((2, CAND * BLOCK, width), jnp.bfloat16),
                pltpu.VMEM((2, width, HEAD), jnp.bfloat16),
                pltpu.VMEM((2, width, HEAD), jnp.bfloat16),
                pltpu.VMEM((2, CAND * BLOCK, 2 * BLOCK), jnp.float32),
                pltpu.VMEM((2, CAND * BLOCK, 2 * BLOCK), jnp.float32),
            ],
        ),
        compiler_params=pltpu.CompilerParams(
            dimension_semantics=("arbitrary", "arbitrary"),
            vmem_limit_bytes=56 * 1024 * 1024,
        ),
        name="attend",
    )(rank, blocks, lens, query_in, grad_out, bias, *bufs)


def swapped(value, axis, stride):
    pairs = [(s, s ^ stride) for s in range(lax.axis_size(axis))]
    return lax.ppermute(value, axis, pairs)


def butterfly(value, axis, stride=1, stop=None):
    stop = lax.axis_size(axis) if stop is None else stop
    while stride < stop:
        value = value + swapped(value, axis, stride)
        stride *= 2
    return value


def quad(value, axis, stride):
    first, second, third = (swapped(value, axis, i * stride) for i in (1, 2, 3))
    return (value + first) + (second + third)


def body(query_in, key_in, value_rows_input, grad_out, query_bias, key_blocks, trace_len):
    n = lax.axis_size("ctx")
    assert n >= 8 and n & (n - 1) == 0
    r = lax.axis_index("ctx")
    traces, _, width_q = query_in.shape
    width_kv = key_in.shape[-1]
    heads = width_kv // HEAD
    group = width_q // width_kv
    exchange, relay = plan(n)
    even = r % 2 == 0
    upper = r & 2 != 0

    halves = jnp.concatenate([key_in, value_rows_input], axis=-1).reshape(
        traces, 2, BLOCK, 2 * heads, HEAD
    )
    low = halves[:, 0].transpose(0, 2, 1, 3)
    high = halves[:, 1].transpose(0, 2, 1, 3)
    low, high, msg_c, msg_d = lax.optimization_barrier(
        (low, high, jnp.where(even, low, high), jnp.where(even, high, low))
    )
    in_c = send(msg_c, exchange["c"])
    in_d = send(msg_d, exchange["d"])
    in_near = send(low, exchange["near"])
    in_far = send(low, exchange["far"])
    low_again = lax.optimization_barrier(low)
    column = jnp.where(r < 2, low_again, jnp.where(r < 6, in_near, in_far))
    bufs_relay = []
    for pairs in relay:
        got = send(column, pairs)
        targets = functools.reduce(jnp.logical_or, [r == b for _, b in pairs])
        column = jnp.where(targets, got, column)
    if relay:
        bufs_relay = [column]
    to_up = jnp.stack([low, jnp.where(even, in_d, in_c)], axis=1)
    to_down = jnp.stack([high, jnp.where(r == n - 1, low, jnp.where(even, in_c, in_d))], axis=1)
    msg_a, msg_b = lax.optimization_barrier(
        (jnp.where(upper, to_down, to_up), jnp.where(upper, to_up, to_down))
    )
    in_a = send(msg_a, exchange["a"])
    in_b = send(msg_b, exchange["b"])
    in_sw = send(column, exchange["swap"])
    bufs = [low, high, in_a, in_b, in_c, in_d, in_near, in_far, in_sw] + bufs_relay

    dq, dbias, own, *outs = attend(
        n,
        heads,
        group,
        r.reshape(1).astype(jnp.int32),
        key_blocks.reshape(-1),
        trace_len,
        query_in,
        grad_out,
        query_bias.reshape(1, -1),
        bufs,
    )
    d_a, d_b, d_c, d_d, d_near, d_far, d_sw = outs[:7]
    f32 = jnp.float32
    bf16 = jnp.bfloat16

    def gate(cond, value):
        return jnp.where(cond, value.astype(f32), 0.0)

    back_a = send_back(d_a, exchange["a"])
    back_b = send_back(d_b, exchange["b"])
    back_sw = send_back(d_sw, exchange["swap"])
    from_up = jnp.where(upper, back_b, back_a).astype(f32)
    from_down = jnp.where(upper, back_a, back_b).astype(f32)
    d_c = (d_c.astype(f32) + jnp.where(even, from_down[:, 1], from_up[:, 1])).astype(bf16)
    d_d = (d_d.astype(f32) + jnp.where(even, from_up[:, 1], from_down[:, 1])).astype(bf16)
    d_near = d_near.astype(f32) + gate((r >= 4) & (r < 6), back_sw)
    d_far = d_far.astype(f32) + gate(r >= n - 2, back_sw)
    low_extra = 0.0
    if relay:
        d_relay = outs[7].astype(f32) + gate((r >= 6) & (r < n - 2), back_sw)
        for pairs in reversed(relay):
            is_from = functools.reduce(jnp.logical_or, [r == b for _, b in pairs])
            got = send_back(jnp.where(is_from, d_relay, 0.0).astype(bf16), pairs)
            low_extra = low_extra + gate(r < 2, got)
            d_near = d_near + gate((r >= 4) & (r < 6), got)
            d_far = d_far + gate(r >= n - 2, got)
            d_relay = d_relay + gate((r >= 6) & (r < n - 2), got)
    back_c = send_back(d_c, exchange["c"])
    back_d = send_back(d_d, exchange["d"])
    back_near = send_back(d_near.astype(bf16), exchange["near"])
    back_far = send_back(d_far.astype(bf16), exchange["far"])

    low_grad = own[:, 0] + from_up[:, 0] + gate(r == n - 1, from_down[:, 1])
    low_grad = low_grad + gate(r == 1, back_sw) + low_extra
    low_grad = low_grad + jnp.where(even, back_c, back_d).astype(f32)
    low_grad = low_grad + back_near.astype(f32) + back_far.astype(f32)
    high_grad = own[:, 1] + from_down[:, 0] + jnp.where(even, back_d, back_c).astype(f32)
    both = jnp.stack([low_grad, high_grad], axis=1).astype(bf16)
    grad_key, grad_value = (
        jnp.concatenate([both[:, :, i, h] for h in range(heads)], axis=-1).reshape(
            traces, 2 * BLOCK, width_kv
        )
        for i in range(2)
    )
    bias_sum = butterfly(quad(butterfly(dbias.reshape(-1), "ctx", 1, 2), "ctx", 2), "ctx", 8)
    if lax.axis_size("dp") == 4:
        bias_total = quad(bias_sum, "dp", 1)
    else:
        bias_total = butterfly(bias_sum, "dp")
    rows = traces * lax.axis_size("dp") * 2 * BLOCK * n
    return dq, grad_key, grad_value, bias_total / math.sqrt(rows)


def solution(mesh):
    return jax.shard_map(
        body,
        mesh=mesh,
        in_specs=(
            P("dp", "ctx", None),
            P("dp", "ctx", None),
            P("dp", "ctx", None),
            P("dp", "ctx", None),
            P(),
            P("dp", None, None),
            P("dp"),
        ),
        out_specs=(P("dp", "ctx", None), P("dp", "ctx", None), P("dp", "ctx", None), P()),
        check_vma=False,
    )
```

```python
import functools
import math

import jax
import jax.numpy as jnp
from jax import lax
from jax.experimental import pallas as pl
from jax.experimental.pallas import tpu as pltpu

from jax.sharding import PartitionSpec as P


HEAD = 128
BLOCK = 128
PROMPT = 2
WINDOW = 3
CAND = PROMPT + WINDOW + 1

LOW, HIGH, A2, A3, B2, B3, C1, D1, NEAR, FAR, SWAP, RELAY = range(12)


def relay_rounds(n):
    known = [0, 2, n // 2 - 1]
    missing = list(range(3, n // 2 - 1))
    rounds = []
    while missing:
        pairs = list(zip(known, missing))
        rounds.append(pairs)
        known = known + [b for _, b in pairs]
        missing = missing[len(pairs) :]
    return rounds


def both_ways(pairs):
    return pairs + [(b, a) for a, b in pairs]


def plan(n):
    exchange = {
        "a": both_ways([(s, s + 2) for s in range(n - 2) if s & 2 == 0]),
        "b": both_ways([(s, s + 2) for s in range(n - 2) if s & 2]),
        "c": both_ways([(s, s + 1) for s in range(0, n, 2)]),
        "d": both_ways([(s, s + 1) for s in range(1, n - 1, 2)]),
        "near": [(0, 4), (1, 5), (n - 1, n - 2)],
        "far": [(0, n - 2), (1, n - 1)],
        "swap": [(1, 0)] + [(s, s ^ 1) for s in range(4, n)],
    }
    relay = [
        [(2 * a + x, 2 * b + x) for a, b in pairs for x in range(2)] for pairs in relay_rounds(n)
    ]
    return exchange, relay


def send(value, pairs):
    return lax.ppermute(value, "ctx", pairs)


def send_back(value, pairs):
    return lax.ppermute(value, "ctx", [(b, a) for a, b in pairs])


def slots(r, n):
    def pick(default, *cases):
        out = default
        for cond, value in reversed(cases):
            out = jnp.where(cond, value, out)
        return out

    even = r % 2 == 0
    upper = r & 2 != 0
    l1, u1 = jnp.where(even, D1, C1), jnp.where(even, C1, D1)
    l2, u2 = jnp.where(upper, A2, B2), jnp.where(upper, B2, A2)
    l3, u3 = jnp.where(upper, A3, B3), jnp.where(upper, B3, A3)
    column = pick(RELAY, (r < 6, NEAR), (r >= n - 2, FAR))
    p0 = pick(
        jnp.where(even, column, SWAP), (r == 0, LOW), (r == 1, l1), (r == 2, l2), (r == 3, l3)
    )
    p1 = pick(
        jnp.where(even, SWAP, column), (r == 0, SWAP), (r == 1, LOW), (r == 2, l1), (r == 3, l2)
    )
    high = [
        HIGH,
        pick(u1, (r == n - 1, LOW)),
        pick(u2, (r == n - 2, NEAR), (r == n - 1, l1)),
        pick(u3, (r == n - 2, LOW), (r == n - 1, l2)),
    ]
    return [p0, p1, LOW, l1, l2, l3], [p0, p1] + high


def attend_kernel(
    n, nbuf, heads, group, rank_ref, blocks_ref, len_ref, q_ref, g_ref, bias_ref, *refs
):
    bufs = refs[:nbuf]
    dq_ref, dbias_ref, own_ref = refs[nbuf : nbuf + 3]
    outs = refs[nbuf + 3 : nbuf + 3 + nbuf - 2]
    kv, acc, probs_buf, ds_buf, q_buf, g_buf, s_buf, dp_buf = refs[nbuf + 3 + nbuf - 2 :]
    t, k = pl.program_id(0), pl.program_id(1)
    r = rank_ref[0]
    scale = HEAD ** (-0.5)
    factor = scale * math.log2(math.e)
    width = 2 * BLOCK
    pairs = group // 2
    nt = (((1,), (1,)), ((), ()))
    part = [slice(c * BLOCK, (c + 1) * BLOCK) for c in range(CAND)]
    places = slots(r, n)

    @pl.when(k == 0)
    def _():
        for i in range(2):
            kv[i] = bufs[i][0]
            for j in range(2):
                kv[A2 + 2 * i + j] = bufs[2 + i][0, j]
        for i in range(4, nbuf):
            kv[i + 2] = bufs[i][0]

    acc[...] = jnp.zeros_like(acc)
    key_pos = lax.broadcasted_iota(jnp.int32, (BLOCK, width), 0)
    query_pos = lax.broadcasted_iota(jnp.int32, (BLOCK, width), 1) % BLOCK
    causal = key_pos <= query_pos

    def fold(op, x):
        return op(x.reshape(BLOCK // 8, 8, width), axis=0)

    keys, keys_t, vals, oks, lives = [], [], [], [], []
    for half in range(2):
        block = 2 * n - 1 - r if half else r
        base = (t * 2 * n + block) * CAND
        ok = []
        for c in range(CAND):
            listed = blocks_ref[base + c] >= 0
            if c < PROMPT:
                listed = listed & (c < block - WINDOW)
            ok.append(listed)
        oks.append(ok)
        lives.append(block * BLOCK + query_pos[:1] < len_ref[t])
        keys.append(jnp.concatenate([kv[s, k] for s in places[half]], axis=0))
        vals.append(jnp.concatenate([kv[s, heads + k] for s in places[half]], axis=0))
        keys_t.append(keys[half].T)

    def load(task):
        half, pair = divmod(task, pairs)
        for g in range(2 * pair, 2 * pair + 2):
            cols = slice(g * HEAD, (g + 1) * HEAD)
            rows = slice(g * BLOCK, (g + 1) * BLOCK)
            here = slice(half * BLOCK, (half + 1) * BLOCK)
            query = q_ref[0, here, cols].astype(jnp.float32) + bias_ref[:, cols]
            q_buf[half, rows] = query.astype(jnp.bfloat16)
            g_buf[half, rows] = g_ref[0, here, cols]

    def products(task):
        half, pair = divmod(task, pairs)
        rows = slice(pair * width, (pair + 1) * width)
        s_buf[task % 2] = lax.dot_general(
            keys[half], q_buf[half, rows], nt, preferred_element_type=jnp.float32
        )
        dp_buf[task % 2] = lax.dot_general(
            vals[half], g_buf[half, rows], nt, preferred_element_type=jnp.float32
        )

    def softmax(task):
        half, pair = divmod(task, pairs)
        span = slice(pair * width, (pair + 1) * width)
        slot = task % 2
        ok = oks[half]
        top = None
        for c in range(CAND):
            x = s_buf[slot, part[c]]
            if c == PROMPT:
                x = jnp.where(causal, x, -1e30)
            x = fold(jnp.max, x)
            if c != PROMPT:
                x = jnp.where(ok[c], x, -1e30)
            top = x if top is None else jnp.maximum(top, x)
        top = jnp.max(top, axis=0, keepdims=True) * factor
        total = jnp.zeros((8, width), jnp.float32)
        for c in range(CAND):
            x = s_buf[slot, part[c]]
            if c == PROMPT:
                e = jnp.exp2(jnp.where(causal, x, -1e30) * factor - top)
            else:
                e = jnp.exp2(x * factor - jnp.where(ok[c], top, 1e30))
            s_buf[slot, part[c]] = e
            total = total + fold(jnp.sum, e)
        total = jnp.sum(total, axis=0, keepdims=True)
        inverse = jnp.where(lives[half], 1.0 / total, 0.0)
        row_dot = jnp.zeros((8, width), jnp.float32)
        for c in range(CAND):
            low = (s_buf[slot, part[c]] * inverse).astype(jnp.bfloat16)
            probs_buf[half, part[c], span] = low
            row_dot = row_dot + fold(jnp.sum, low.astype(jnp.float32) * dp_buf[slot, part[c]])
        row_dot = jnp.sum(row_dot, axis=0, keepdims=True)
        for c in range(CAND):
            probs = s_buf[slot, part[c]] * inverse
            ds_buf[half, part[c], span] = (probs * (dp_buf[slot, part[c]] - row_dot)).astype(
                jnp.bfloat16
            )

    def query_grad(task):
        half, pair = divmod(task, pairs)
        span = slice(pair * width, (pair + 1) * width)
        here = slice(half * BLOCK, (half + 1) * BLOCK)
        dq = scale * jnp.dot(
            keys_t[half], ds_buf[half, :, span], preferred_element_type=jnp.float32
        )
        for i in range(2):
            cols = slice((2 * pair + i) * HEAD, (2 * pair + i + 1) * HEAD)
            dq_head = dq[:, i * BLOCK : (i + 1) * BLOCK].T
            dq_ref[0, here, cols] = dq_head.astype(jnp.bfloat16)
            row = jnp.sum(dq_head, axis=0, keepdims=True)
            if half == 0:
                dbias_ref[:, cols] = jnp.where(t == 0, 0.0, dbias_ref[:, cols]) + row
            else:
                dbias_ref[:, cols] += row

    def key_grad(task, count, which=(0, 1)):
        half, pair = divmod(task, pairs)
        span = slice((pair - count + 1) * width, (pair + 1) * width)
        for value in which:
            if value:
                grad = jnp.dot(
                    probs_buf[half, :, span], g_buf[half, span], preferred_element_type=jnp.float32
                )
            else:
                grad = scale * jnp.dot(
                    ds_buf[half, :, span], q_buf[half, span], preferred_element_type=jnp.float32
                )
            for c in range(CAND):
                acc[places[half][c], value] += grad[part[c]]

    tasks = 2 * pairs
    load(0)
    products(0)
    for task in range(tasks):
        if task + 1 < tasks:
            load(task + 1)
            products(task + 1)
        if task > 0:
            query_grad(task - 1)
            if task % 2 == 0:
                key_grad(task - 1, 2, (1,))
            elif task > 1:
                key_grad(task - 2, 2, (0,))
        softmax(task)
    query_grad(tasks - 1)
    key_grad(tasks - 1, 2)

    for i in range(2):
        own_ref[0, i, :, 0] = acc[i]
    for i in range(2):
        for j in range(2):
            outs[i][0, j, :, 0] = acc[A2 + 2 * i + j].astype(jnp.bfloat16)
    for i in range(2, nbuf - 2):
        outs[i][0, :, 0] = acc[i + 4].astype(jnp.bfloat16)


def attend(n, heads, group, rank, blocks, lens, query_in, grad_out, bias, bufs):
    traces = query_in.shape[0]
    nbuf = len(bufs)
    width = group * HEAD
    row_spec = pl.BlockSpec((1, 2 * BLOCK, width), lambda t, k, *_: (t, 0, k))
    bias_spec = pl.BlockSpec((1, width), lambda t, k, *_: (0, k))
    buf_spec = pl.BlockSpec((1, 2 * heads, BLOCK, HEAD), lambda t, k, *_: (t, 0, 0, 0))
    own_spec = pl.BlockSpec((1, 2, 2, 1, BLOCK, HEAD), lambda t, k, *_: (t, 0, 0, k, 0, 0))
    out_spec = pl.BlockSpec((1, 2, 1, BLOCK, HEAD), lambda t, k, *_: (t, 0, k, 0, 0))
    two_spec = pl.BlockSpec((1, 2, 2 * heads, BLOCK, HEAD), lambda t, k, *_: (t, 0, 0, 0, 0))
    two_out = pl.BlockSpec((1, 2, 2, 1, BLOCK, HEAD), lambda t, k, *_: (t, 0, 0, k, 0, 0))
    out_shape = [
        jax.ShapeDtypeStruct(query_in.shape, jnp.bfloat16),
        jax.ShapeDtypeStruct((1, heads * width), jnp.float32),
        jax.ShapeDtypeStruct((traces, 2, 2, heads, BLOCK, HEAD), jnp.float32),
    ]
    out_shape += [jax.ShapeDtypeStruct((traces, 2, 2, heads, BLOCK, HEAD), jnp.bfloat16)] * 2
    out_shape += [jax.ShapeDtypeStruct((traces, 2, heads, BLOCK, HEAD), jnp.bfloat16)] * (nbuf - 4)
    return pl.pallas_call(
        functools.partial(attend_kernel, n, nbuf, heads, group),
        out_shape=out_shape,
        grid_spec=pltpu.PrefetchScalarGridSpec(
            num_scalar_prefetch=3,
            grid=(traces, heads),
            in_specs=[row_spec, row_spec, bias_spec]
            + [buf_spec] * 2
            + [two_spec] * 2
            + [buf_spec] * (nbuf - 4),
            out_specs=[row_spec, bias_spec, own_spec]
            + [two_out] * 2
            + [out_spec] * (nbuf - 4),
            scratch_shapes=[
                pltpu.VMEM((nbuf + 2, 2 * heads, BLOCK, HEAD), jnp.bfloat16),
                pltpu.VMEM((nbuf + 2, 2, BLOCK, HEAD), jnp.float32),
                pltpu.VMEM((2, CAND * BLOCK, width), jnp.bfloat16),
                pltpu.VMEM((2, CAND * BLOCK, width), jnp.bfloat16),
                pltpu.VMEM((2, width, HEAD), jnp.bfloat16),
                pltpu.VMEM((2, width, HEAD), jnp.bfloat16),
                pltpu.VMEM((2, CAND * BLOCK, 2 * BLOCK), jnp.float32),
                pltpu.VMEM((2, CAND * BLOCK, 2 * BLOCK), jnp.float32),
            ],
        ),
        compiler_params=pltpu.CompilerParams(
            dimension_semantics=("arbitrary", "arbitrary"),
            vmem_limit_bytes=56 * 1024 * 1024,
        ),
        name="attend",
    )(rank, blocks, lens, query_in, grad_out, bias, *bufs)


def swapped(value, axis, stride):
    pairs = [(s, s ^ stride) for s in range(lax.axis_size(axis))]
    return lax.ppermute(value, axis, pairs)


def butterfly(value, axis, stride=1, stop=None):
    stop = lax.axis_size(axis) if stop is None else stop
    while stride < stop:
        value = value + swapped(value, axis, stride)
        stride *= 2
    return value


def quad(value, axis, stride):
    first, second, third = (swapped(value, axis, i * stride) for i in (1, 2, 3))
    return (value + first) + (second + third)


def body(query_in, key_in, value_rows_input, grad_out, query_bias, key_blocks, trace_len):
    n = lax.axis_size("ctx")
    assert n >= 8 and n & (n - 1) == 0
    r = lax.axis_index("ctx")
    traces, _, width_q = query_in.shape
    width_kv = key_in.shape[-1]
    heads = width_kv // HEAD
    group = width_q // width_kv
    exchange, relay = plan(n)
    even = r % 2 == 0
    upper = r & 2 != 0

    halves = jnp.concatenate([key_in, value_rows_input], axis=-1).reshape(
        traces, 2, BLOCK, 2 * heads, HEAD
    )
    low = halves[:, 0].transpose(0, 2, 1, 3)
    high = halves[:, 1].transpose(0, 2, 1, 3)
    low, high, msg_c, msg_d = lax.optimization_barrier(
        (low, high, jnp.where(even, low, high), jnp.where(even, high, low))
    )
    in_c = send(msg_c, exchange["c"])
    in_d = send(msg_d, exchange["d"])
    in_near = send(low, exchange["near"])
    in_far = send(low, exchange["far"])
    low_again = lax.optimization_barrier(low)
    column = jnp.where(r < 2, low_again, jnp.where(r < 6, in_near, in_far))
    bufs_relay = []
    for pairs in relay:
        got = send(column, pairs)
        targets = functools.reduce(jnp.logical_or, [r == b for _, b in pairs])
        column = jnp.where(targets, got, column)
    if relay:
        bufs_relay = [column]
    to_up = jnp.stack([low, jnp.where(even, in_d, in_c)], axis=1)
    to_down = jnp.stack([high, jnp.where(r == n - 1, low, jnp.where(even, in_c, in_d))], axis=1)
    msg_a, msg_b = lax.optimization_barrier(
        (jnp.where(upper, to_down, to_up), jnp.where(upper, to_up, to_down))
    )
    in_a = send(msg_a, exchange["a"])
    in_b = send(msg_b, exchange["b"])
    in_sw = send(column, exchange["swap"])
    bufs = [low, high, in_a, in_b, in_c, in_d, in_near, in_far, in_sw] + bufs_relay

    dq, dbias, own, *outs = attend(
        n,
        heads,
        group,
        r.reshape(1).astype(jnp.int32),
        key_blocks.reshape(-1),
        trace_len,
        query_in,
        grad_out,
        query_bias.reshape(1, -1),
        bufs,
    )
    d_a, d_b, d_c, d_d, d_near, d_far, d_sw = outs[:7]
    f32 = jnp.float32
    bf16 = jnp.bfloat16

    def gate(cond, value):
        return jnp.where(cond, value.astype(f32), 0.0)

    back_a = send_back(d_a, exchange["a"])
    back_b = send_back(d_b, exchange["b"])
    back_sw = send_back(d_sw, exchange["swap"])
    from_up = jnp.where(upper, back_b, back_a).astype(f32)
    from_down = jnp.where(upper, back_a, back_b).astype(f32)
    same = even == upper
    further_a, further_b = back_a[:, 1], back_b[:, 1]
    d_c = (d_c.astype(f32) + jnp.where(same, further_a, further_b).astype(f32)).astype(bf16)
    d_d = (d_d.astype(f32) + jnp.where(same, further_b, further_a).astype(f32)).astype(bf16)
    d_near = d_near.astype(f32) + gate((r >= 4) & (r < 6), back_sw)
    d_far = d_far.astype(f32) + gate(r >= n - 2, back_sw)
    low_extra = 0.0
    if relay:
        d_relay = outs[7].astype(f32) + gate((r >= 6) & (r < n - 2), back_sw)
        for pairs in reversed(relay):
            is_from = functools.reduce(jnp.logical_or, [r == b for _, b in pairs])
            got = send_back(jnp.where(is_from, d_relay, 0.0).astype(bf16), pairs)
            low_extra = low_extra + gate(r < 2, got)
            d_near = d_near + gate((r >= 4) & (r < 6), got)
            d_far = d_far + gate(r >= n - 2, got)
            d_relay = d_relay + gate((r >= 6) & (r < n - 2), got)
    back_c = send_back(d_c, exchange["c"])
    back_d = send_back(d_d, exchange["d"])
    back_near = send_back(d_near.astype(bf16), exchange["near"])
    back_far = send_back(d_far.astype(bf16), exchange["far"])

    low_grad = own[:, 0] + from_up[:, 0] + gate(r == n - 1, from_down[:, 1])
    low_grad = low_grad + gate(r == 1, back_sw) + low_extra
    low_grad = low_grad + jnp.where(even, back_c, back_d).astype(f32)
    low_grad = low_grad + back_near.astype(f32) + back_far.astype(f32)
    high_grad = own[:, 1] + from_down[:, 0] + jnp.where(even, back_d, back_c).astype(f32)
    both = jnp.stack([low_grad, high_grad], axis=1).astype(bf16)
    grad_key, grad_value = (
        jnp.concatenate([both[:, :, i, h] for h in range(heads)], axis=-1).reshape(
            traces, 2 * BLOCK, width_kv
        )
        for i in range(2)
    )
    bias_sum = butterfly(quad(butterfly(dbias.reshape(-1), "ctx", 1, 2), "ctx", 2), "ctx", 8)
    if lax.axis_size("dp") == 4:
        bias_total = quad(bias_sum, "dp", 1)
    else:
        bias_total = butterfly(bias_sum, "dp")
    rows = traces * lax.axis_size("dp") * 2 * BLOCK * n
    return dq, grad_key, grad_value, bias_total / math.sqrt(rows)


def solution(mesh):
    return jax.shard_map(
        body,
        mesh=mesh,
        in_specs=(
            P("dp", "ctx", None),
            P("dp", "ctx", None),
            P("dp", "ctx", None),
            P("dp", "ctx", None),
            P(),
            P("dp", None, None),
            P("dp"),
        ),
        out_specs=(P("dp", "ctx", None), P("dp", "ctx", None), P("dp", "ctx", None), P()),
        check_vma=False,
    )
```
